256 devices in a mesh: users: 16 (over x, y), ctx: 16 (over z, core).
Axes of the slice: x: 4, y: 4, z: 8, core: 2. Of those that a mesh axis runs over, the one named last changes fastest.
Arguments:
- cand_feat: bfloat16 [98304, 1024], P(('users', 'ctx')), may hold values from -27 to 27
- cand_user: int32 [98304, 1], P(('users', 'ctx')), may hold values from 0 to 15; in each aligned block of 384 rows (0 to 383, 384 to 767, ...) at most 48 rows name the same one
- hist_kv: bfloat16 [1, 16, 2048, 2048], P(None, 'users', 'ctx'), may hold values from -27 to 27
- hist_mask: int32 [16, 16], P('users'), may hold values from 0 to 1, as said below
- gain_in: float32 [1, 1024], replicated, may hold values from 0.25 to 1.75
- w_uq: bfloat16 [1, 1024, 2048], replicated, may hold values from -0.1875 to 0.1875
- gain_attn: float32 [1, 1024], replicated, may hold values from 0.25 to 1.75
- w_out: bfloat16 [1, 1024, 1024], replicated, may hold values from -0.1875 to 0.1875
Outputs:
- cand_out: bfloat16 [98304, 1024], P(('users', 'ctx'))
The draws below stay inside these ranges and needn't reach their ends.
Inputs may be any that keep to these rules, and one draw needn't show every extreme that they name: `cand_user`: within the rows of one device no user is named by more than 48 rows, a bound that some block reaches of them. `hist_mask`: every user has exactly 8 ones among its 16 blocks.
All inputs are finite; a program needn't handle non-finite values.
Results may differ from the reference program's by a relative error of at most 0.0039.
Values may be sent and summed in bfloat16 or wider, within the bound.
A program may use at most 128 MiB of HBM per device.

```python
import math
import jax
import jax.numpy as jnp
import numpy as np
from jax import lax

D = 1024
H = 8
BLK = 128
LAYERS = 1
SRC_ROWS = 384
USERS = 16
ROWS = 98304
HIST = 2048
NBLK = 16
LIVE = 8
MOST = 48
USER_CAP = 12288


def log_scale(key, shape):
    return jnp.exp(jax.random.uniform(key, shape, jnp.float32, math.log(0.3), math.log(3.0)))


def draw_cand_feat(key, part):
    key_main = jax.random.fold_in(key, 0)
    key_rows = jax.random.fold_in(key, 2)
    key_cols = jax.random.fold_in(key, 3)
    noise = jnp.clip(jax.random.normal(key_main, (ROWS, D), jnp.float32), -3.0, 3.0)
    scaled = noise * log_scale(key_rows, (ROWS, 1)) * log_scale(key_cols, (1, D))
    return scaled.astype(jnp.bfloat16)


def draw_hist_kv(key, part):
    key_main = jax.random.fold_in(key, 0)
    key_rows = jax.random.fold_in(key, 2)
    key_cols = jax.random.fold_in(key, 3)
    full_shape = (LAYERS, USERS, HIST, 2 * D)
    noise = jnp.clip(jax.random.normal(key_main, full_shape, jnp.float32), -3.0, 3.0)
    is_value = jnp.arange(2 * D) >= D
    column_scale = jnp.where(is_value, log_scale(key_cols, (2 * D,)), 1.0)
    row_scale = jnp.where(is_value, log_scale(key_rows, (LAYERS, USERS, HIST, 1)), 1.0)
    return (noise * column_scale * row_scale).astype(jnp.bfloat16)


def draw_hist_mask(key, part):
    user_keys = jax.random.split(key, USERS)
    orders = jax.vmap(lambda user_key: jax.random.permutation(user_key, NBLK))(user_keys)
    return (orders < LIVE).astype(jnp.int32)


def assign_block(stream_key, own, number, rows, count, top, reach, lean):
    ranking = jax.random.permutation(stream_key, count)
    crowded, ordinary = portions_of(count, rows * top, reach, lean, True), portions_of(count, rows * top, reach, lean, False)
    places = jnp.arange(count)

    def named(lengths, offset_by):
        used = int((lengths > 0).sum())
        fixed = max(1, used // 4)
        passed = fixed + (places - fixed + offset_by * (used - fixed)) % max(1, count - fixed)
        return jnp.zeros((count,), jnp.int32).at[ranking[jnp.where(places < fixed, places, passed)]].set(jnp.asarray(lengths, jnp.int32))

    lengths = jnp.where(number % 4 == 0, named(crowded, number // 4), named(ordinary, number - number // 4 - 1))
    mixed = jax.random.permutation(jax.random.fold_in(own, 3), count)
    donor, taker = mixed[0:count // 2 * 2:2], mixed[1:count // 2 * 2:2]
    slack = jnp.minimum(lengths[donor] - 1, reach - lengths[taker]) // 2
    slack = jnp.where((donor == ranking[0]) | (taker == ranking[0]) | (lengths[taker] == 0), 0, jnp.maximum(slack, 0))
    passed = jax.random.randint(jax.random.fold_in(own, 4), (count // 2,), 0, 1 << 20) % (slack + 1)
    lengths = lengths.at[donor].add(-passed).at[taker].add(passed)
    items = jnp.searchsorted(jnp.cumsum(lengths), jnp.arange(rows * top), side="right").astype(jnp.int32)
    table = items.reshape(top, rows).T
    table = table[jax.random.permutation(jax.random.fold_in(own, 1), rows)]
    offset_by = jax.random.randint(jax.random.fold_in(own, 2), (rows, 1), 0, top)
    return jnp.take_along_axis(table, (jnp.arange(top)[None, :] + offset_by) % top, axis=1)


def portions_of(amount, total, limit, slope, full):
    weights = [(1 << 20) // math.isqrt(standing ** slope) + 1 for standing in range(1, amount + 1)]
    largest = limit if full else min(limit, max(-(-total // amount), total * weights[0] // sum(weights)))
    least = 1 if total - largest >= amount - 1 else 0
    counts, rest = [largest] + [least] * (amount - 1), total - largest - least * (amount - 1)
    while rest > 0:
        candidates = [i for i in range(1, amount) if counts[i] < largest] or [i for i in range(1, amount) if counts[i] < limit]
        pool, remaining = sum([weights[i] for i in candidates]), rest
        for i in candidates:
            addition = min(limit - counts[i], max(1, remaining * weights[i] // pool), rest)
            counts[i] = counts[i] + addition
            rest = rest - addition
    return np.array(counts)


def bell_draw(key, dims, scale, bound, kind=jnp.bfloat16):
    entries = jax.random.normal(key, dims, jnp.float32) * scale
    return jnp.minimum(jnp.maximum(entries, -bound), bound).astype(kind)


def setup_inputs(seed: int = 0) -> dict:
    splits = jax.random.split(jax.random.key(seed), 9)
    cand_feat = draw_cand_feat(jax.random.fold_in(splits[8], 71), 0)
    cand_user_keys = jax.random.split(jax.random.fold_in(splits[1], 1), ROWS // SRC_ROWS)
    cand_user_turns = jax.random.permutation(jax.random.fold_in(splits[1], 3), ROWS // SRC_ROWS)
    cand_user = jax.vmap(lambda own, number: assign_block(jax.random.fold_in(splits[1], 2), own, number, SRC_ROWS, USERS, 1, MOST, 2))(cand_user_keys, cand_user_turns).reshape((ROWS, 1))
    hist_kv = draw_hist_kv(jax.random.fold_in(splits[8], 71), 0)
    hist_mask = draw_hist_mask(jax.random.fold_in(splits[8], 71), 0)
    gain_in = jnp.clip(1.0 + 0.15 * jax.random.normal(splits[4], (LAYERS, D), jnp.float32), 0.25, 1.75)
    w_uq = bell_draw(splits[5], (LAYERS, D, 2 * D), D ** -0.5, 0.1875)
    gain_attn = jnp.clip(1.0 + 0.15 * jax.random.normal(splits[6], (LAYERS, D), jnp.float32), 0.25, 1.75)
    w_out = bell_draw(splits[7], (LAYERS, D, D), D ** -0.5, 0.1875)
    return dict(cand_feat=cand_feat, cand_user=cand_user, hist_kv=hist_kv, hist_mask=hist_mask, gain_in=gain_in, w_uq=w_uq, gain_attn=gain_attn, w_out=w_out)


def centred_norm(inputs):
    middle = lax.optimization_barrier(jnp.mean(inputs, axis=-1, keepdims=True))
    shifted = inputs - middle
    spread = lax.optimization_barrier(jnp.mean(shifted * shifted, axis=-1, keepdims=True))
    return shifted * lax.rsqrt(spread + 1e-05)

def score_user(queries, kv_rows):
    capacity = queries.shape[0]
    head_size = D // H
    query_heads = queries.reshape(capacity, H, head_size).transpose(1, 0, 2)
    key_heads = kv_rows[:, :D].reshape(-1, H, head_size).transpose(1, 0, 2)
    value_heads = kv_rows[:, D:].reshape(-1, H, head_size).transpose(1, 0, 2)

    def one_head(packed):
        query_part, key_part, value_part = packed
        scores = jnp.dot(query_part, key_part.T, preferred_element_type=jnp.float32) * head_size ** (-0.5)
        attn_weights = jax.nn.silu(scores).astype(jnp.bfloat16)
        return jnp.dot(attn_weights, value_part, preferred_element_type=jnp.float32)
    combined = lax.map(one_head, (query_heads, key_heads, value_heads))
    return combined.transpose(1, 0, 2).reshape(capacity, D)

def reference(cand_feat, cand_user, hist_kv, hist_mask, gain_in, w_uq, gain_attn, w_out):
    owner_ids = cand_user[:, 0]
    user_range = jnp.arange(USERS, dtype=jnp.int32)
    sorted_rows = jnp.argsort(owner_ids, stable=True).astype(jnp.int32)
    user_counts = lax.optimization_barrier(jnp.sum((owner_ids[:, None] == user_range[None, :]).astype(jnp.int32), axis=0)).astype(jnp.int32)
    user_starts = (jnp.cumsum(user_counts) - user_counts).astype(jnp.int32)
    slot_offsets = jnp.arange(USER_CAP, dtype=jnp.int32)
    positions = jnp.minimum(user_starts[:, None] + slot_offsets[None, :], ROWS - 1).astype(jnp.int32)
    members = sorted_rows[positions]
    in_range = (slot_offsets[None, :] < user_counts[:, None]).astype(jnp.float32)
    live_blocks = jnp.argsort(1 - hist_mask, axis=1, stable=True)[:, :LIVE].astype(jnp.int32)
    hidden = cand_feat
    for layer_index in range(LAYERS):
        residual = hidden.astype(jnp.float32)
        normed = (centred_norm(residual) * gain_in[layer_index]).astype(jnp.bfloat16)
        projected = jnp.dot(normed, w_uq[layer_index], preferred_element_type=jnp.float32)
        gate_vals = jax.nn.silu(projected[:, :D])
        queries = jax.nn.silu(projected[:, D:]).astype(jnp.bfloat16)
        layer_kv = hist_kv[layer_index]

        def add_user(user_index, running):
            picked = queries[members[user_index]]
            user_kv = layer_kv[user_index].reshape(NBLK, BLK, 2 * D)[live_blocks[user_index]].reshape(LIVE * BLK, 2 * D)
            scored = score_user(picked, user_kv) * in_range[user_index][:, None]
            return running.at[members[user_index]].add(scored)
        attended = lax.fori_loop(0, USERS, add_user, jnp.zeros((ROWS, D), jnp.float32))
        mixed = (centred_norm(attended) * gain_attn[layer_index] * gate_vals).astype(jnp.bfloat16)
        hidden = (residual + jnp.dot(mixed, w_out[layer_index], preferred_element_type=jnp.float32)).astype(jnp.bfloat16)
    return hidden
```

```python
import jax
import jax.numpy as jnp
from jax import lax
from jax.experimental import pallas as pl
from jax.experimental.pallas import tpu as pltpu
from jax.sharding import PartitionSpec as P

H = 8
HD = 128
D = H * HD
BLK = 128
LIVE = 8
ROWS = 384
USERS = 16
CTX = 16
RING = 8
CAP = 48
SLOTS = USERS * CAP
HALF = LIVE * BLK // 2
GROUPS = ((0,), (1, 2), (3, 4), (5, 6), (7,))
MESH = pl.DeviceIdType.MESH
F32 = jnp.float32
BF16 = jnp.bfloat16


def silu(v):
    half = 0.5 * v
    return half + half * jnp.tanh(half)


def partner_user(me_u, d):
    step = lax.rem(d * 7, USERS)
    nx = lax.rem(lax.div(me_u, 4) + lax.div(step, 4), 4)
    ny = lax.rem(lax.rem(me_u, 4) + lax.rem(step, 4), 4)
    return nx * 4 + ny


def slot_rows(user):
    return pl.ds(pl.multiple_of(user * CAP, CAP), CAP)


def kernel(
    x_hbm, usr_ref, kv_hbm, mask_ref, gin_ref, wuq_hbm, gattn_ref, wout_hbm, out_ref,
    xv, wq, wg, wo, landed, kv, normed, qh, qs, qr, asend, arecv, acc, att, gate, disp, comb,
    lsem, a_send, a_recv, q_send, q_recv, t_send, t_recv,
    r_send, l_send, s_send, r_recv, l_recv, so_recv, sr_recv, sl_recv,
):
    me_u = lax.axis_index("users")
    me_c = lax.axis_index("ctx")
    z = lax.div(me_c, 2)
    core = lax.rem(me_c, 2)

    def column_of(ctx):
        return pl.multiple_of(lax.rem(ctx, 2) * D + lax.div(ctx, 2) * HD, HD)

    load_x = pltpu.make_async_copy(x_hbm, xv, lsem.at[0])
    load_wq = pltpu.make_async_copy(wuq_hbm.at[0, :, pl.ds(D, D)], wq, lsem.at[1])
    load_wg = pltpu.make_async_copy(wuq_hbm.at[0, :, pl.ds(0, D)], wg, lsem.at[2])
    load_wo = pltpu.make_async_copy(wout_hbm.at[0], wo, lsem.at[3])
    load_own = pltpu.make_async_copy(
        kv_hbm.at[0, 0, :, pl.ds(column_of(me_c), HD)], landed.at[me_c], lsem.at[4]
    )
    for load in (load_x, load_wq, load_own, load_wg, load_wo):
        load.start()

    barrier = pltpu.get_barrier_semaphore()

    def greet(d, carry):
        pl.semaphore_signal(
            barrier, inc=1, device_id={"ctx": lax.rem(me_c + d, CTX)}, device_id_type=MESH
        )
        pl.semaphore_signal(
            barrier, inc=1, device_id={"users": lax.rem(me_u + d, USERS)}, device_id_type=MESH
        )
        return carry

    lax.fori_loop(1, 16, greet, 0)
    pl.semaphore_wait(barrier, 30)

    def send_block(d, carry):
        dst = lax.rem(me_c + lax.rem(d * 7, CTX), CTX)
        pltpu.make_async_remote_copy(
            src_ref=kv_hbm.at[0, 0, :, pl.ds(column_of(dst), HD)],
            dst_ref=landed.at[me_c],
            send_sem=a_send,
            recv_sem=a_recv,
            device_id={"ctx": dst},
            device_id_type=MESH,
        ).start()
        return carry

    lax.fori_loop(1, CTX, send_block, 0)

    users = usr_ref[...]
    one_hot = (users == lax.broadcasted_iota(jnp.int32, (ROWS, 128), 1)).astype(F32)
    row_id = lax.broadcasted_iota(jnp.int32, (ROWS, ROWS), 0)
    col_id = lax.broadcasted_iota(jnp.int32, (ROWS, ROWS), 1)
    before = (col_id < row_id).astype(F32).astype(BF16)
    earlier = jnp.dot(before, one_hot.astype(BF16), preferred_element_type=F32)
    rank = jnp.sum(earlier * one_hot, axis=1, keepdims=True)
    slot = users.astype(F32) * CAP + rank
    slot_row = jnp.sum(jnp.where(row_id == col_id, slot, 0.0), axis=0, keepdims=True)
    comb[...] = (
        (lax.broadcasted_iota(jnp.int32, (ROWS, SLOTS), 1).astype(F32) == slot)
        .astype(F32).astype(BF16)
    )
    disp[...] = (
        (lax.broadcasted_iota(jnp.int32, (SLOTS, ROWS), 0).astype(F32) == slot_row)
        .astype(F32).astype(BF16)
    )

    load_x.wait()

    def norm_rows(t, carry):
        rows = pl.ds(pl.multiple_of(t * 64, 64), 64)
        value = xv[rows, :].astype(F32)
        shifted = value - jnp.mean(value, axis=1, keepdims=True)
        spread = jnp.mean(shifted * shifted, axis=1, keepdims=True)
        normed[rows, :] = (shifted * lax.rsqrt(spread + 1e-05) * gin_ref[...]).astype(BF16)
        return carry

    lax.fori_loop(0, ROWS // 64, norm_rows, 0)
    load_wq.wait()

    def project_query(n, carry):
        cols = pl.ds(pl.multiple_of(n * 256, 256), 256)
        value = silu(jnp.dot(normed[...], wq[:, cols], preferred_element_type=F32)).astype(BF16)
        qh[2 * n] = value[:, :HD]
        qh[2 * n + 1] = value[:, HD:]
        return carry

    lax.fori_loop(0, H // 2, project_query, 0)

    def head_at(order):
        offset = 0 if order == 0 else (-((order + 1) // 2) if order % 2 else order // 2)
        return lax.rem(z + (offset + RING), RING)

    def exchange(group, source, target, send_sem, recv_sem):
        first, count = group[0], len(group)

        def send(d, carry):
            dst = partner_user(me_u, d)
            pltpu.make_async_remote_copy(
                src_ref=source.at[pl.ds(first, count), slot_rows(dst), :],
                dst_ref=target.at[pl.ds(first, count), slot_rows(me_u), :],
                send_sem=send_sem,
                recv_sem=recv_sem,
                device_id={"users": dst},
                device_id_type=MESH,
            ).start()
            return carry

        lax.fori_loop(1, USERS, send, 0)
        for order in group:
            target[order, slot_rows(me_u), :] = source[order, slot_rows(me_u), :]

    def exchange_wait(group, buffer, sem):
        part = buffer.at[pl.ds(group[0], len(group)), pl.ds(0, SLOTS - CAP), :]
        pltpu.make_async_copy(part, part, sem).wait()

    for g, group in enumerate(GROUPS):
        heads = [qh[head_at(order)] for order in group]
        picked = heads[0] if len(group) == 1 else jnp.concatenate(heads, axis=1)
        routed = jnp.dot(disp[...], picked, preferred_element_type=F32).astype(BF16)
        for at, order in enumerate(group):
            qs[order] = routed[:, at * HD:(at + 1) * HD]
        exchange(group, qs, qr, q_send.at[g], q_recv.at[g])

    load_wg.wait()

    def project_gate(n, carry):
        cols = pl.ds(pl.multiple_of(n * 256, 256), 256)
        gate[:, cols] = silu(jnp.dot(normed[...], wg[:, cols], preferred_element_type=F32))
        return carry

    lax.fori_loop(0, H // 2, project_gate, 0)

    counts = []
    running = jnp.int32(0)
    for b in range(CTX):
        running = running + mask_ref[0, b]
        counts.append(running)
    load_own.wait()
    got = landed.at[pl.ds(0, CTX - 1)]
    pltpu.make_async_copy(got, got, a_recv).wait()

    def piece(lane, head, half):
        return lane * 2 * RING + head * 2 + half

    for r in range(LIVE):
        block = jnp.int32(0)
        for b in range(CTX):
            block = block + (counts[b] <= r).astype(jnp.int32)
        block = jnp.minimum(block, CTX - 1)
        kv[piece(core, z, r // 4), pl.ds((r % 4) * BLK, BLK), :] = landed[block]

    right = {"ctx": lax.rem(z + 1, RING) * 2 + core}
    left = {"ctx": lax.rem(z + RING - 1, RING) * 2 + core}
    sibling = {"ctx": z * 2 + 1 - core}

    def pass_on(at, to, send_sem, recv_sem):
        pltpu.make_async_remote_copy(
            src_ref=kv.at[at], dst_ref=kv.at[at], send_sem=send_sem, recv_sem=recv_sem,
            device_id=to, device_id_type=MESH,
        ).start()

    def arrived(at, sem):
        pltpu.make_async_copy(kv.at[at], kv.at[at], sem).wait()

    pass_on(piece(core, z, 0), right, r_send, r_recv.at[0])
    pass_on(piece(core, z, 1), left, l_send, l_recv.at[0])
    pass_on(piece(core, z, 0), sibling, s_send, so_recv.at[0])
    pass_on(piece(core, z, 1), sibling, s_send, so_recv.at[1])
    pass_on(piece(core, z, 1), right, r_send, r_recv.at[1])
    pass_on(piece(core, z, 0), left, l_send, l_recv.at[1])

    scale = 0.5 * HD ** (-0.5)
    row_tile = 384

    def attend(order, half, opening):
        head = head_at(order)
        key_at, value_at = piece(0, head, half), piece(1, head, half)

        def rows_of(t, carry):
            rows = pl.ds(pl.multiple_of(t * row_tile, row_tile), row_tile)
            scores = lax.dot_general(
                qr[order, rows, :], kv[key_at], (((1,), (1,)), ((), ())),
                preferred_element_type=F32,
            ) * scale
            weights = (scores + scores * jnp.tanh(scores)).astype(BF16)
            value = jnp.dot(weights, kv[value_at], preferred_element_type=F32)
            if opening:
                acc[order, rows, :] = value
            else:
                asend[order, rows, :] = (acc[order, rows, :] + value).astype(BF16)
            return carry

        lax.fori_loop(0, SLOTS // row_tile, rows_of, 0)

    def send_attended(g):
        exchange(GROUPS[g], asend, arecv, t_send.at[g], t_recv.at[g])

    exchange_wait(GROUPS[0], qr, q_recv.at[0])
    for half in range(2):
        arrived(piece(1 - core, z, half), so_recv.at[half])
        attend(0, half, half == 0)
    send_attended(0)

    def units_of(i):
        s, first = i // 2 + 1, i % 2
        if s == 4:
            return ((7, 0), (7, 1))
        return ((2 * s - 1, first), (2 * s, 1 - first))

    def finish(i):
        s = i // 2 + 1
        opening = i % 2 == 0
        if opening:
            exchange_wait(GROUPS[s], qr, q_recv.at[s])
        (lo, lo_half), (hi, hi_half) = units_of(i)
        arrived(piece(1 - core, head_at(lo), lo_half), sr_recv.at[i])
        attend(lo, lo_half, opening)
        arrived(piece(1 - core, head_at(hi), hi_half), sl_recv.at[i])
        attend(hi, hi_half, opening and s < 4)
        if not opening or s == 4:
            send_attended(s)

    for i in range(7):
        (lo, lo_half), (hi, hi_half) = units_of(i)
        from_left = piece(core, head_at(lo), lo_half)
        from_right = piece(core, head_at(hi), hi_half)
        onward = i + 2 if i < 5 else None
        arrived(from_left, r_recv.at[i])
        if onward is not None and (onward < 6 or i == 4):
            pass_on(from_left, right, r_send, r_recv.at[onward])
        pass_on(from_left, sibling, s_send, sr_recv.at[i])
        arrived(from_right, l_recv.at[i])
        if onward is not None and (onward < 6 or i == 4):
            pass_on(from_right, left, l_send, l_recv.at[onward])
        pass_on(from_right, sibling, s_send, sl_recv.at[i])
        if i > 0:
            finish(i - 1)
    finish(6)

    for g, group in enumerate(GROUPS):
        exchange_wait(group, arecv, t_recv.at[g])
        parts = [arecv[order] for order in group]
        packed = parts[0] if len(group) == 1 else jnp.concatenate(parts, axis=1)
        own = jnp.dot(comb[...], packed, preferred_element_type=F32)
        for at, order in enumerate(group):
            att[head_at(order)] = own[:, at * HD:(at + 1) * HD]

    def mix_rows(t, carry):
        rows = pl.ds(pl.multiple_of(t * 64, 64), 64)
        value = jnp.concatenate([att[h, rows, :] for h in range(H)], axis=1)
        shifted = value - jnp.mean(value, axis=1, keepdims=True)
        spread = jnp.mean(shifted * shifted, axis=1, keepdims=True)
        normed[rows, :] = (
            shifted * lax.rsqrt(spread + 1e-05) * gattn_ref[...] * gate[rows, :]
        ).astype(BF16)
        return carry

    lax.fori_loop(0, ROWS // 64, mix_rows, 0)
    load_wo.wait()

    def project_out(n, carry):
        cols = pl.ds(pl.multiple_of(n * 256, 256), 256)
        value = jnp.dot(normed[...], wo[:, cols], preferred_element_type=F32)
        out_ref[:, cols] = (xv[:, cols].astype(F32) + value).astype(BF16)
        return carry

    lax.fori_loop(0, D // 256, project_out, 0)

    sent = landed.at[pl.ds(0, CTX - 1)]
    pltpu.make_async_copy(sent, sent, a_send).wait()
    for g, group in enumerate(GROUPS):
        exchange_wait(group, qs, q_send.at[g])
        exchange_wait(group, asend, t_send.at[g])
    for sem, count in ((r_send, 7), (l_send, 7), (s_send, 16)):
        moved = kv.at[pl.ds(0, count)]
        pltpu.make_async_copy(moved, moved, sem).wait()


def on_device(cand_feat, cand_user, hist_kv, hist_mask, gain_in, w_uq, gain_attn, w_out):
    anywhere = pl.BlockSpec(memory_space=pl.ANY)
    vmem = pl.BlockSpec(memory_space=pltpu.VMEM)
    dma = pltpu.SemaphoreType.DMA
    return pl.pallas_call(
        kernel,
        out_shape=jax.ShapeDtypeStruct((ROWS, D), BF16),
        in_specs=[
            anywhere, vmem, anywhere, pl.BlockSpec(memory_space=pltpu.SMEM),
            vmem, anywhere, vmem, anywhere,
        ],
        out_specs=vmem,
        scratch_shapes=[
            pltpu.VMEM((ROWS, D), BF16),
            pltpu.VMEM((D, D), BF16),
            pltpu.VMEM((D, D), BF16),
            pltpu.VMEM((D, D), BF16),
            pltpu.VMEM((CTX, BLK, HD), BF16),
            pltpu.VMEM((2 * 2 * RING, HALF, HD), BF16),
            pltpu.VMEM((ROWS, D), BF16),
            pltpu.VMEM((H, ROWS, HD), BF16),
            pltpu.VMEM((H, SLOTS, HD), BF16),
            pltpu.VMEM((H, SLOTS, HD), BF16),
            pltpu.VMEM((H, SLOTS, HD), BF16),
            pltpu.VMEM((H, SLOTS, HD), BF16),
            pltpu.VMEM((H, SLOTS, HD), F32),
            pltpu.VMEM((H, ROWS, HD), F32),
            pltpu.VMEM((ROWS, D), F32),
            pltpu.VMEM((SLOTS, ROWS), BF16),
            pltpu.VMEM((ROWS, SLOTS), BF16),
            dma((5,)), dma(()), dma(()), dma((5,)), dma((5,)), dma((5,)), dma((5,)),
            dma(()), dma(()), dma(()), dma((7,)), dma((7,)), dma((2,)), dma((7,)), dma((7,)),
        ],
        compiler_params=pltpu.CompilerParams(
            collective_id=0, has_side_effects=True, vmem_limit_bytes=56 * 1024 * 1024
        ),
    )(cand_feat, cand_user, hist_kv, hist_mask, gain_in, w_uq, gain_attn, w_out)


def solution(mesh):
    in_specs = (
        P(("users", "ctx"), None),
        P(("users", "ctx"), None),
        P(None, "users", "ctx", None),
        P("users", None),
        P(),
        P(),
        P(),
        P(),
    )
    out_specs = P(("users", "ctx"), None)
    return jax.shard_map(
        on_device, mesh=mesh, in_specs=in_specs, out_specs=out_specs, check_vma=False
    )
```

```python
import jax
import jax.numpy as jnp
from jax import lax
from jax.experimental import pallas as pl
from jax.experimental.pallas import tpu as pltpu
from jax.sharding import PartitionSpec as P

H = 8
HD = 128
D = H * HD
BLK = 128
LIVE = 8
ROWS = 384
USERS = 16
CTX = 16
RING = 8
CAP = 48
SLOTS = USERS * CAP
HALF = LIVE * BLK // 2
GROUPS = ((0,), (1, 2), (3, 4), (5, 6), (7,))
MESH = pl.DeviceIdType.MESH
F32 = jnp.float32
BF16 = jnp.bfloat16


def silu(v):
    half = 0.5 * v
    return half + half * jnp.tanh(half)


def partner_user(me_u, d):
    step = lax.rem(d * 7, USERS)
    nx = lax.rem(lax.div(me_u, 4) + lax.div(step, 4), 4)
    ny = lax.rem(lax.rem(me_u, 4) + lax.rem(step, 4), 4)
    return nx * 4 + ny


def slot_rows(user):
    return pl.ds(pl.multiple_of(user * CAP, CAP), CAP)


def kernel(
    x_hbm, usr_ref, kv_hbm, mask_ref, gin_ref, wuq_hbm, gattn_ref, mixed_ref,
    xv, wq, wg, landed_a, landed_b, kv, normed, qs, qr, asend, arecv, acc, att, gate, disp, comb,
    lsem, wsem, a_send, a_recv, q_send, q_recv, t_send, t_recv,
    r_send, l_send, s_send, r_recv, l_recv, so_recv, sr_recv, sl_recv,
):
    me_u = lax.axis_index("users")
    me_c = lax.axis_index("ctx")
    z = lax.div(me_c, 2)
    core = lax.rem(me_c, 2)

    def column_of(ctx):
        return pl.multiple_of(lax.rem(ctx, 2) * D + lax.div(ctx, 2) * HD, HD)

    def head_at(order):
        offset = 0 if order == 0 else (-((order + 1) // 2) if order % 2 else order // 2)
        return lax.rem(z + (offset + RING), RING)

    def load_query_weight(order):
        column = pl.multiple_of(D + head_at(order) * HD, HD)
        return pltpu.make_async_copy(
            wuq_hbm.at[0, :, pl.ds(column, HD)], wq.at[order], wsem.at[order]
        )

    load_x = pltpu.make_async_copy(x_hbm, xv, lsem.at[0])
    load_wg = pltpu.make_async_copy(wuq_hbm.at[0, :, pl.ds(0, D)], wg, lsem.at[1])
    landed = (landed_a, landed_b)

    def half_rows(half):
        return pl.ds(half * (BLK // 2), BLK // 2)

    def load_own(half):
        return pltpu.make_async_copy(
            kv_hbm.at[0, 0, half_rows(half), pl.ds(column_of(me_c), HD)],
            landed[half].at[me_c],
            lsem.at[2 + half],
        )

    load_x.start()
    for order in range(H):
        load_query_weight(order).start()
    for half in range(2):
        load_own(half).start()
    load_wg.start()

    barrier = pltpu.get_barrier_semaphore()

    def greet(d, carry):
        pl.semaphore_signal(
            barrier, inc=1, device_id={"ctx": lax.rem(me_c + d, CTX)}, device_id_type=MESH
        )
        pl.semaphore_signal(
            barrier, inc=1, device_id={"users": lax.rem(me_u + d, USERS)}, device_id_type=MESH
        )
        return carry

    lax.fori_loop(1, 16, greet, 0)
    pl.semaphore_wait(barrier, 30)

    def send_blocks(half):
        def send(d, carry):
            dst = lax.rem(me_c + lax.rem(d * 7, CTX), CTX)
            pltpu.make_async_remote_copy(
                src_ref=kv_hbm.at[0, 0, half_rows(half), pl.ds(column_of(dst), HD)],
                dst_ref=landed[half].at[me_c],
                send_sem=a_send.at[half],
                recv_sem=a_recv.at[half],
                device_id={"ctx": dst},
                device_id_type=MESH,
            ).start()
            return carry

        lax.fori_loop(1, CTX, send, 0)

    def blocks_wait(half, sem):
        got = landed[half].at[pl.ds(0, CTX - 1)]
        pltpu.make_async_copy(got, got, sem.at[half]).wait()

    send_blocks(0)
    send_blocks(1)

    row_id = lax.broadcasted_iota(jnp.int32, (ROWS, ROWS), 0)
    col_id = lax.broadcasted_iota(jnp.int32, (ROWS, ROWS), 1)
    users = jnp.sum(
        jnp.where(row_id == col_id, usr_ref[...].astype(F32), 0.0), axis=1, keepdims=True
    )
    one_hot = (users == lax.broadcasted_iota(jnp.int32, (ROWS, 128), 1).astype(F32)).astype(F32)
    before = (col_id < row_id).astype(F32).astype(BF16)
    earlier = jnp.dot(before, one_hot.astype(BF16), preferred_element_type=F32)
    rank = jnp.sum(earlier * one_hot, axis=1, keepdims=True)
    slot = users * CAP + rank
    slot_row = jnp.sum(jnp.where(row_id == col_id, slot, 0.0), axis=0, keepdims=True)
    comb[...] = (
        (lax.broadcasted_iota(jnp.int32, (ROWS, SLOTS), 1).astype(F32) == slot)
        .astype(F32).astype(BF16)
    )
    disp[...] = (
        (lax.broadcasted_iota(jnp.int32, (SLOTS, ROWS), 0).astype(F32) == slot_row)
        .astype(F32).astype(BF16)
    )

    load_x.wait()

    def norm_rows(t, carry):
        rows = pl.ds(pl.multiple_of(t * 64, 64), 64)
        value = xv[rows, :].astype(F32)
        shifted = value - jnp.mean(value, axis=1, keepdims=True)
        spread = jnp.mean(shifted * shifted, axis=1, keepdims=True)
        normed[rows, :] = (shifted * lax.rsqrt(spread + 1e-05) * gin_ref[...]).astype(BF16)
        return carry

    lax.fori_loop(0, ROWS // 64, norm_rows, 0)
    def exchange(group, source, target, send_sem, recv_sem):
        first, count = group[0], len(group)

        def send(d, carry):
            dst = partner_user(me_u, d)
            pltpu.make_async_remote_copy(
                src_ref=source.at[pl.ds(first, count), slot_rows(dst), :],
                dst_ref=target.at[pl.ds(first, count), slot_rows(me_u), :],
                send_sem=send_sem,
                recv_sem=recv_sem,
                device_id={"users": dst},
                device_id_type=MESH,
            ).start()
            return carry

        lax.fori_loop(1, USERS, send, 0)
        for order in group:
            target[order, slot_rows(me_u), :] = source[order, slot_rows(me_u), :]

    def exchange_wait(group, buffer, sem):
        part = buffer.at[pl.ds(group[0], len(group)), pl.ds(0, SLOTS - CAP), :]
        pltpu.make_async_copy(part, part, sem).wait()

    for g, group in enumerate(GROUPS):
        for order in group:
            load_query_weight(order).wait()
        weights = [wq[order] for order in group]
        weight = weights[0] if len(group) == 1 else jnp.concatenate(weights, axis=1)
        query = silu(jnp.dot(normed[...], weight, preferred_element_type=F32)).astype(BF16)
        routed = jnp.dot(disp[...], query, preferred_element_type=F32).astype(BF16)
        for at, order in enumerate(group):
            qs[order] = routed[:, at * HD:(at + 1) * HD]
        exchange(group, qs, qr, q_send.at[g], q_recv.at[g])

    load_wg.wait()

    def project_gate(n, carry):
        cols = pl.ds(pl.multiple_of(n * 256, 256), 256)
        gate[:, cols] = silu(jnp.dot(normed[...], wg[:, cols], preferred_element_type=F32))
        return carry

    lax.fori_loop(0, H // 2, project_gate, 0)

    counts = []
    running = jnp.int32(0)
    for b in range(CTX):
        running = running + mask_ref[0, b]
        counts.append(running)
    live = []
    for r in range(LIVE):
        block = jnp.int32(0)
        for b in range(CTX):
            block = block + (counts[b] <= r).astype(jnp.int32)
        live.append(jnp.minimum(block, CTX - 1))

    def piece(lane, head, half):
        return lane * 2 * RING + head * 2 + half

    right = {"ctx": lax.rem(z + 1, RING) * 2 + core}
    left = {"ctx": lax.rem(z + RING - 1, RING) * 2 + core}
    sibling = {"ctx": z * 2 + 1 - core}

    def pass_on(at, to, send_sem, recv_sem):
        pltpu.make_async_remote_copy(
            src_ref=kv.at[at], dst_ref=kv.at[at], send_sem=send_sem, recv_sem=recv_sem,
            device_id=to, device_id_type=MESH,
        ).start()

    def arrived(at, sem):
        pltpu.make_async_copy(kv.at[at], kv.at[at], sem).wait()

    for half in range(2):
        load_own(half).wait()
        blocks_wait(half, a_recv)
        own = piece(core, z, half)
        for r in range(LIVE):
            kv[own, pl.ds(r * (BLK // 2), BLK // 2), :] = landed[half][live[r]]
        pass_on(own, right, r_send, r_recv.at[half])
        pass_on(own, left, l_send, l_recv.at[half])
        pass_on(own, sibling, s_send, so_recv.at[half])

    scale = 0.5 * HD ** (-0.5)
    row_tile = 384

    def attend(order, half, opening):
        head = head_at(order)
        key_at, value_at = piece(0, head, half), piece(1, head, half)

        def rows_of(t, carry):
            rows = pl.ds(pl.multiple_of(t * row_tile, row_tile), row_tile)
            scores = lax.dot_general(
                qr[order, rows, :], kv[key_at], (((1,), (1,)), ((), ())),
                preferred_element_type=F32,
            ) * scale
            weights = (scores + scores * jnp.tanh(scores)).astype(BF16)
            value = jnp.dot(weights, kv[value_at], preferred_element_type=F32)
            if opening:
                acc[order, rows, :] = value
            else:
                asend[order, rows, :] = (acc[order, rows, :] + value).astype(BF16)
            return carry

        lax.fori_loop(0, SLOTS // row_tile, rows_of, 0)

    def send_attended(g):
        exchange(GROUPS[g], asend, arecv, t_send.at[g], t_recv.at[g])

    exchange_wait(GROUPS[0], qr, q_recv.at[0])
    for half in range(2):
        arrived(piece(1 - core, z, half), so_recv.at[half])
        attend(0, half, half == 0)
    send_attended(0)

    def units_of(i):
        s, first = i // 2 + 1, i % 2
        if s == 4:
            return ((7, 0), (7, 1))
        return ((2 * s - 1, first), (2 * s, first))

    def finish(i):
        s = i // 2 + 1
        opening = i % 2 == 0
        if opening:
            exchange_wait(GROUPS[s], qr, q_recv.at[s])
        (lo, lo_half), (hi, hi_half) = units_of(i)
        arrived(piece(1 - core, head_at(lo), lo_half), sr_recv.at[i])
        attend(lo, lo_half, opening)
        arrived(piece(1 - core, head_at(hi), hi_half), sl_recv.at[i])
        attend(hi, hi_half, opening and s < 4)
        if not opening or s == 4:
            send_attended(s)

    for i in range(7):
        (lo, lo_half), (hi, hi_half) = units_of(i)
        from_left = piece(core, head_at(lo), lo_half)
        from_right = piece(core, head_at(hi), hi_half)
        arrived(from_left, r_recv.at[i])
        if i < 5:
            pass_on(from_left, right, r_send, r_recv.at[i + 2])
        pass_on(from_left, sibling, s_send, sr_recv.at[i])
        arrived(from_right, l_recv.at[i])
        if i < 4 or i == 5:
            pass_on(from_right, left, l_send, l_recv.at[min(i + 2, 6)])
        pass_on(from_right, sibling, s_send, sl_recv.at[i])
        if i > 0:
            finish(i - 1)
    finish(6)

    for g, group in enumerate(GROUPS):
        exchange_wait(group, arecv, t_recv.at[g])
        parts = [arecv[order] for order in group]
        packed = parts[0] if len(group) == 1 else jnp.concatenate(parts, axis=1)
        own = jnp.dot(comb[...], packed, preferred_element_type=F32)
        for at, order in enumerate(group):
            att[head_at(order)] = own[:, at * HD:(at + 1) * HD]

    def mix_rows(t, carry):
        rows = pl.ds(pl.multiple_of(t * 64, 64), 64)
        value = jnp.concatenate([att[h, rows, :] for h in range(H)], axis=1)
        shifted = value - jnp.mean(value, axis=1, keepdims=True)
        spread = jnp.mean(shifted * shifted, axis=1, keepdims=True)
        mixed_ref[rows, :] = (
            shifted * lax.rsqrt(spread + 1e-05) * gattn_ref[...] * gate[rows, :]
        ).astype(BF16)
        return carry

    lax.fori_loop(0, ROWS // 64, mix_rows, 0)
    for half in range(2):
        blocks_wait(half, a_send)
    for g, group in enumerate(GROUPS):
        exchange_wait(group, qs, q_send.at[g])
        exchange_wait(group, asend, t_send.at[g])
    for sem, count in ((r_send, 7), (l_send, 7), (s_send, 16)):
        moved = kv.at[pl.ds(0, count)]
        pltpu.make_async_copy(moved, moved, sem).wait()


def on_device(cand_feat, cand_user, hist_kv, hist_mask, gain_in, w_uq, gain_attn, w_out):
    anywhere = pl.BlockSpec(memory_space=pl.ANY)
    vmem = pl.BlockSpec(memory_space=pltpu.VMEM)
    dma = pltpu.SemaphoreType.DMA
    mixed = pl.pallas_call(
        kernel,
        out_shape=jax.ShapeDtypeStruct((ROWS, D), BF16),
        in_specs=[
            anywhere, vmem, anywhere, pl.BlockSpec(memory_space=pltpu.SMEM),
            vmem, anywhere, vmem,
        ],
        out_specs=vmem,
        scratch_shapes=[
            pltpu.VMEM((ROWS, D), BF16),
            pltpu.VMEM((H, D, HD), BF16),
            pltpu.VMEM((D, D), BF16),
            pltpu.VMEM((CTX, BLK // 2, HD), BF16),
            pltpu.VMEM((CTX, BLK // 2, HD), BF16),
            pltpu.VMEM((2 * 2 * RING, HALF, HD), BF16),
            pltpu.VMEM((ROWS, D), BF16),
            pltpu.VMEM((H, SLOTS, HD), BF16),
            pltpu.VMEM((H, SLOTS, HD), BF16),
            pltpu.VMEM((H, SLOTS, HD), BF16),
            pltpu.VMEM((H, SLOTS, HD), BF16),
            pltpu.VMEM((H, SLOTS, HD), F32),
            pltpu.VMEM((H, ROWS, HD), F32),
            pltpu.VMEM((ROWS, D), F32),
            pltpu.VMEM((SLOTS, ROWS), BF16),
            pltpu.VMEM((ROWS, SLOTS), BF16),
            dma((4,)), dma((H,)), dma((2,)), dma((2,)), dma((5,)), dma((5,)), dma((5,)), dma((5,)),
            dma(()), dma(()), dma(()), dma((7,)), dma((7,)), dma((2,)), dma((7,)), dma((7,)),
        ],
        compiler_params=pltpu.CompilerParams(
            collective_id=0, has_side_effects=True, vmem_limit_bytes=56 * 1024 * 1024
        ),
    )(cand_feat, cand_user.reshape(1, ROWS), hist_kv, hist_mask, gain_in, w_uq, gain_attn)
    scored = jnp.dot(mixed, w_out[0], preferred_element_type=F32)
    return (cand_feat.astype(F32) + scored).astype(BF16)


def solution(mesh):
    in_specs = (
        P(("users", "ctx"), None),
        P(("users", "ctx"), None),
        P(None, "users", "ctx", None),
        P("users", None),
        P(),
        P(),
        P(),
        P(),
    )
    out_specs = P(("users", "ctx"), None)
    return jax.shard_map(
        on_device, mesh=mesh, in_specs=in_specs, out_specs=out_specs, check_vma=False
    )
```

```python
import jax
import jax.numpy as jnp
from jax import lax
from jax.experimental import pallas as pl
from jax.experimental.pallas import tpu as pltpu
from jax.sharding import PartitionSpec as P

H = 8
HD = 128
D = H * HD
BLK = 128
LIVE = 8
ROWS = 384
USERS = 16
CTX = 16
RING = 8
CAP = 48
SLOTS = USERS * CAP
HALF = LIVE * BLK // 2
GROUPS = ((0,), (1, 2), (3, 4), (5, 6), (7,))
MESH = pl.DeviceIdType.MESH
F32 = jnp.float32
BF16 = jnp.bfloat16


def silu(v):
    half = 0.5 * v
    return half + half * jnp.tanh(half)


def partner_user(me_u, d):
    step = lax.rem(d * 7, USERS)
    nx = lax.rem(lax.div(me_u, 4) + lax.div(step, 4), 4)
    ny = lax.rem(lax.rem(me_u, 4) + lax.rem(step, 4), 4)
    return nx * 4 + ny


def slot_rows(user):
    return pl.ds(pl.multiple_of(user * CAP, CAP), CAP)


def kernel(
    x_hbm, usr_ref, kv_hbm, mask_ref, gin_ref, wuq_hbm, gattn_ref, mixed_ref,
    xv, wq, wg, landed_a, landed_b, kv, normed, qs, qr, asend, arecv, acc, att, gate, disp, comb,
    lsem, wsem, a_send, a_recv, q_send, q_recv, t_send, t_recv,
    r_send, l_send, s_send, r_recv, l_recv, so_recv, sr_recv, sl_recv,
):
    me_u = lax.axis_index("users")
    me_c = lax.axis_index("ctx")
    z = lax.div(me_c, 2)
    core = lax.rem(me_c, 2)

    def column_of(ctx):
        return pl.multiple_of(lax.rem(ctx, 2) * D + lax.div(ctx, 2) * HD, HD)

    def head_at(order):
        offset = 0 if order == 0 else (-((order + 1) // 2) if order % 2 else order // 2)
        return lax.rem(z + (offset + RING), RING)

    def load_query_weight(order):
        column = pl.multiple_of(D + head_at(order) * HD, HD)
        return pltpu.make_async_copy(
            wuq_hbm.at[0, :, pl.ds(column, HD)], wq.at[order], wsem.at[order]
        )

    load_x = pltpu.make_async_copy(x_hbm, xv, lsem.at[0])
    load_wg = pltpu.make_async_copy(wuq_hbm.at[0, :, pl.ds(0, D)], wg, lsem.at[1])
    landed = (landed_a, landed_b)

    def half_rows(half):
        return pl.ds(half * (BLK // 2), BLK // 2)

    def load_own(half):
        return pltpu.make_async_copy(
            kv_hbm.at[0, 0, half_rows(half), pl.ds(column_of(me_c), HD)],
            landed[half].at[me_c],
            lsem.at[2 + half],
        )

    load_x.start()
    for order in range(H):
        load_query_weight(order).start()
    for half in range(2):
        load_own(half).start()
    load_wg.start()

    barrier = pltpu.get_barrier_semaphore()

    def greet(d, carry):
        pl.semaphore_signal(
            barrier, inc=1, device_id={"ctx": lax.rem(me_c + d, CTX)}, device_id_type=MESH
        )
        pl.semaphore_signal(
            barrier, inc=1, device_id={"users": lax.rem(me_u + d, USERS)}, device_id_type=MESH
        )
        return carry

    lax.fori_loop(1, 16, greet, 0)
    pl.semaphore_wait(barrier, 30)

    def send_blocks(half):
        def send(d, carry):
            dst = lax.rem(me_c + lax.rem(d * 7, CTX), CTX)
            pltpu.make_async_remote_copy(
                src_ref=kv_hbm.at[0, 0, half_rows(half), pl.ds(column_of(dst), HD)],
                dst_ref=landed[half].at[me_c],
                send_sem=a_send.at[half],
                recv_sem=a_recv.at[half],
                device_id={"ctx": dst},
                device_id_type=MESH,
            ).start()
            return carry

        lax.fori_loop(1, CTX, send, 0)

    def blocks_wait(half, sem):
        got = landed[half].at[pl.ds(0, CTX - 1)]
        pltpu.make_async_copy(got, got, sem.at[half]).wait()

    send_blocks(0)

    row_id = lax.broadcasted_iota(jnp.int32, (ROWS, ROWS), 0)
    col_id = lax.broadcasted_iota(jnp.int32, (ROWS, ROWS), 1)
    users = jnp.sum(
        jnp.where(row_id == col_id, usr_ref[...].astype(F32), 0.0), axis=1, keepdims=True
    )
    one_hot = (users == lax.broadcasted_iota(jnp.int32, (ROWS, 128), 1).astype(F32)).astype(F32)
    before = (col_id < row_id).astype(F32).astype(BF16)
    earlier = jnp.dot(before, one_hot.astype(BF16), preferred_element_type=F32)
    rank = jnp.sum(earlier * one_hot, axis=1, keepdims=True)
    slot = users * CAP + rank
    slot_row = jnp.sum(jnp.where(row_id == col_id, slot, 0.0), axis=0, keepdims=True)
    comb[...] = (
        (lax.broadcasted_iota(jnp.int32, (ROWS, SLOTS), 1).astype(F32) == slot)
        .astype(F32).astype(BF16)
    )
    disp[...] = (
        (lax.broadcasted_iota(jnp.int32, (SLOTS, ROWS), 0).astype(F32) == slot_row)
        .astype(F32).astype(BF16)
    )

    load_x.wait()

    def norm_rows(t, carry):
        rows = pl.ds(pl.multiple_of(t * 64, 64), 64)
        value = xv[rows, :].astype(F32)
        shifted = value - jnp.mean(value, axis=1, keepdims=True)
        spread = jnp.mean(shifted * shifted, axis=1, keepdims=True)
        normed[rows, :] = (shifted * lax.rsqrt(spread + 1e-05) * gin_ref[...]).astype(BF16)
        return carry

    lax.fori_loop(0, ROWS // 64, norm_rows, 0)
    def exchange(group, source, target, send_sem, recv_sem):
        first, count = group[0], len(group)

        def send(d, carry):
            dst = partner_user(me_u, d)
            pltpu.make_async_remote_copy(
                src_ref=source.at[pl.ds(first, count), slot_rows(dst), :],
                dst_ref=target.at[pl.ds(first, count), slot_rows(me_u), :],
                send_sem=send_sem,
                recv_sem=recv_sem,
                device_id={"users": dst},
                device_id_type=MESH,
            ).start()
            return carry

        lax.fori_loop(1, USERS, send, 0)
        for order in group:
            target[order, slot_rows(me_u), :] = source[order, slot_rows(me_u), :]

    def exchange_wait(group, buffer, sem):
        part = buffer.at[pl.ds(group[0], len(group)), pl.ds(0, SLOTS - CAP), :]
        pltpu.make_async_copy(part, part, sem).wait()

    def route_queries(g):
        group = GROUPS[g]
        for order in group:
            load_query_weight(order).wait()
        weights = [wq[order] for order in group]
        weight = weights[0] if len(group) == 1 else jnp.concatenate(weights, axis=1)
        query = silu(jnp.dot(normed[...], weight, preferred_element_type=F32)).astype(BF16)
        routed = jnp.dot(disp[...], query, preferred_element_type=F32).astype(BF16)
        for at, order in enumerate(group):
            qs[order] = routed[:, at * HD:(at + 1) * HD]

    def send_queries(g):
        exchange(GROUPS[g], qs, qr, q_send.at[g], q_recv.at[g])

    route_queries(0)
    send_queries(0)
    route_queries(1)
    send_queries(1)
    blocks_wait(0, a_send)
    send_blocks(1)
    route_queries(2)
    load_wg.wait()

    def project_gate(n, carry):
        cols = pl.ds(pl.multiple_of(n * 256, 256), 256)
        gate[:, cols] = silu(jnp.dot(normed[...], wg[:, cols], preferred_element_type=F32))
        return carry

    lax.fori_loop(0, H // 2, project_gate, 0)

    counts = []
    running = jnp.int32(0)
    for b in range(CTX):
        running = running + mask_ref[0, b]
        counts.append(running)
    live = []
    for r in range(LIVE):
        block = jnp.int32(0)
        for b in range(CTX):
            block = block + (counts[b] <= r).astype(jnp.int32)
        live.append(jnp.minimum(block, CTX - 1))

    def piece(lane, head, half):
        return lane * 2 * RING + head * 2 + half

    right = {"ctx": lax.rem(z + 1, RING) * 2 + core}
    left = {"ctx": lax.rem(z + RING - 1, RING) * 2 + core}
    sibling = {"ctx": z * 2 + 1 - core}

    def pass_on(at, to, send_sem, recv_sem):
        pltpu.make_async_remote_copy(
            src_ref=kv.at[at], dst_ref=kv.at[at], send_sem=send_sem, recv_sem=recv_sem,
            device_id=to, device_id_type=MESH,
        ).start()

    def arrived(at, sem):
        pltpu.make_async_copy(kv.at[at], kv.at[at], sem).wait()

    for half in range(2):
        load_own(half).wait()
        blocks_wait(half, a_recv)
        own = piece(core, z, half)
        for r in range(LIVE):
            kv[own, pl.ds(r * (BLK // 2), BLK // 2), :] = landed[half][live[r]]
        pass_on(own, right, r_send, r_recv.at[half])
        pass_on(own, left, l_send, l_recv.at[half])
        pass_on(own, sibling, s_send, so_recv.at[half])
        if half == 0:
            send_queries(2)
            route_queries(3)
            route_queries(4)
    send_queries(3)
    send_queries(4)

    scale = 0.5 * HD ** (-0.5)

    def attend(order, half, opening):
        head = head_at(order)
        scores = lax.dot_general(
            qr[order], kv[piece(0, head, half)], (((1,), (1,)), ((), ())),
            preferred_element_type=F32,
        ) * scale
        weights = (scores + scores * jnp.tanh(scores)).astype(BF16)
        value = jnp.dot(weights, kv[piece(1, head, half)], preferred_element_type=F32)
        if opening:
            acc[order] = value
        else:
            asend[order] = (acc[order] + value).astype(BF16)

    def send_attended(g):
        exchange(GROUPS[g], asend, arecv, t_send.at[g], t_recv.at[g])

    def finish_first():
        exchange_wait(GROUPS[0], qr, q_recv.at[0])
        for half in range(2):
            arrived(piece(1 - core, z, half), so_recv.at[half])
            attend(0, half, half == 0)
        send_attended(0)

    def units_of(i):
        s, first = i // 2 + 1, i % 2
        if s == 4:
            return ((7, 0), (7, 1))
        return ((2 * s - 1, first), (2 * s, first))

    def finish(i):
        s = i // 2 + 1
        opening = i % 2 == 0
        if opening:
            exchange_wait(GROUPS[s], qr, q_recv.at[s])
        (lo, lo_half), (hi, hi_half) = units_of(i)
        arrived(piece(1 - core, head_at(lo), lo_half), sr_recv.at[i])
        attend(lo, lo_half, opening)
        arrived(piece(1 - core, head_at(hi), hi_half), sl_recv.at[i])
        attend(hi, hi_half, opening and s < 4)
        if not opening or s == 4:
            send_attended(s)

    for i in range(7):
        (lo, lo_half), (hi, hi_half) = units_of(i)
        from_left = piece(core, head_at(lo), lo_half)
        from_right = piece(core, head_at(hi), hi_half)
        arrived(from_left, r_recv.at[i])
        if i < 5:
            pass_on(from_left, right, r_send, r_recv.at[i + 2])
        pass_on(from_left, sibling, s_send, sr_recv.at[i])
        arrived(from_right, l_recv.at[i])
        if i < 4 or i == 5:
            pass_on(from_right, left, l_send, l_recv.at[min(i + 2, 6)])
        pass_on(from_right, sibling, s_send, sl_recv.at[i])
        if i == 0:
            finish_first()
        elif i < 6:
            finish(i - 1)
        if i == 5:
            finish(5)
    finish(6)

    for g, group in enumerate(GROUPS):
        exchange_wait(group, arecv, t_recv.at[g])
        parts = [arecv[order] for order in group]
        packed = parts[0] if len(group) == 1 else jnp.concatenate(parts, axis=1)
        own = jnp.dot(comb[...], packed, preferred_element_type=F32)
        for at, order in enumerate(group):
            att[head_at(order)] = own[:, at * HD:(at + 1) * HD]

    def mix_rows(t, carry):
        rows = pl.ds(pl.multiple_of(t * 64, 64), 64)
        value = jnp.concatenate([att[h, rows, :] for h in range(H)], axis=1)
        shifted = value - jnp.mean(value, axis=1, keepdims=True)
        spread = jnp.mean(shifted * shifted, axis=1, keepdims=True)
        mixed_ref[rows, :] = (
            shifted * lax.rsqrt(spread + 1e-05) * gattn_ref[...] * gate[rows, :]
        ).astype(BF16)
        return carry

    lax.fori_loop(0, ROWS // 64, mix_rows, 0)
    blocks_wait(1, a_send)
    for g, group in enumerate(GROUPS):
        exchange_wait(group, qs, q_send.at[g])
        exchange_wait(group, asend, t_send.at[g])
    for sem, count in ((r_send, 7), (l_send, 7), (s_send, 16)):
        moved = kv.at[pl.ds(0, count)]
        pltpu.make_async_copy(moved, moved, sem).wait()


def on_device(cand_feat, cand_user, hist_kv, hist_mask, gain_in, w_uq, gain_attn, w_out):
    anywhere = pl.BlockSpec(memory_space=pl.ANY)
    vmem = pl.BlockSpec(memory_space=pltpu.VMEM)
    dma = pltpu.SemaphoreType.DMA
    mixed = pl.pallas_call(
        kernel,
        out_shape=jax.ShapeDtypeStruct((ROWS, D), BF16),
        in_specs=[
            anywhere, vmem, anywhere, pl.BlockSpec(memory_space=pltpu.SMEM),
            vmem, anywhere, vmem,
        ],
        out_specs=vmem,
        scratch_shapes=[
            pltpu.VMEM((ROWS, D), BF16),
            pltpu.VMEM((H, D, HD), BF16),
            pltpu.VMEM((D, D), BF16),
            pltpu.VMEM((CTX, BLK // 2, HD), BF16),
            pltpu.VMEM((CTX, BLK // 2, HD), BF16),
            pltpu.VMEM((2 * 2 * RING, HALF, HD), BF16),
            pltpu.VMEM((ROWS, D), BF16),
            pltpu.VMEM((H, SLOTS, HD), BF16),
            pltpu.VMEM((H, SLOTS, HD), BF16),
            pltpu.VMEM((H, SLOTS, HD), BF16),
            pltpu.VMEM((H, SLOTS, HD), BF16),
            pltpu.VMEM((H, SLOTS, HD), F32),
            pltpu.VMEM((H, ROWS, HD), F32),
            pltpu.VMEM((ROWS, D), F32),
            pltpu.VMEM((SLOTS, ROWS), BF16),
            pltpu.VMEM((ROWS, SLOTS), BF16),
            dma((4,)), dma((H,)), dma((2,)), dma((2,)), dma((5,)), dma((5,)), dma((5,)), dma((5,)),
            dma(()), dma(()), dma(()), dma((7,)), dma((7,)), dma((2,)), dma((7,)), dma((7,)),
        ],
        compiler_params=pltpu.CompilerParams(
            collective_id=0, has_side_effects=True, vmem_limit_bytes=56 * 1024 * 1024
        ),
    )(cand_feat, cand_user.reshape(1, ROWS), hist_kv, hist_mask, gain_in, w_uq, gain_attn)
    scored = jnp.dot(mixed, w_out[0], preferred_element_type=F32)
    return (cand_feat.astype(F32) + scored).astype(BF16)


def solution(mesh):
    in_specs = (
        P(("users", "ctx"), None),
        P(("users", "ctx"), None),
        P(None, "users", "ctx", None),
        P("users", None),
        P(),
        P(),
        P(),
        P(),
    )
    out_specs = P(("users", "ctx"), None)
    return jax.shard_map(
        on_device, mesh=mesh, in_specs=in_specs, out_specs=out_specs, check_vma=False
    )
```

```python
import jax
import jax.numpy as jnp
from jax import lax
from jax.experimental import pallas as pl
from jax.experimental.pallas import tpu as pltpu
from jax.sharding import PartitionSpec as P

H = 8
HD = 128
D = H * HD
BLK = 128
LIVE = 8
ROWS = 384
USERS = 16
CTX = 16
RING = 8
CAP = 48
SLOTS = USERS * CAP
HALF = LIVE * BLK // 2
GROUPS = ((0,), (1, 2), (3, 4), (5, 6), (7,))
MESH = pl.DeviceIdType.MESH
F32 = jnp.float32
BF16 = jnp.bfloat16


def silu(v):
    half = 0.5 * v
    return half + half * jnp.tanh(half)


def partner_user(me_u, d):
    step = lax.rem(d * 7, USERS)
    nx = lax.rem(lax.div(me_u, 4) + lax.div(step, 4), 4)
    ny = lax.rem(lax.rem(me_u, 4) + lax.rem(step, 4), 4)
    return nx * 4 + ny


def slot_rows(user):
    return pl.ds(pl.multiple_of(user * CAP, CAP), CAP)


def kernel(
    x_hbm, usr_ref, kv_hbm, mask_ref, gin_ref, wuq_hbm, gattn_ref, mixed_ref,
    xv, wq, wg, landed_a, landed_b, kv, normed, qs, qr, asend, arecv, acc, att, gate, disp, comb,
    lsem, wsem, a_send, a_recv, q_send, q_recv, t_send, t_recv,
    r_send, l_send, s_send, r_recv, l_recv, so_recv, sr_recv, sl_recv,
):
    me_u = lax.axis_index("users")
    me_c = lax.axis_index("ctx")
    z = lax.div(me_c, 2)
    core = lax.rem(me_c, 2)

    def column_of(ctx):
        return pl.multiple_of(lax.rem(ctx, 2) * D + lax.div(ctx, 2) * HD, HD)

    def head_at(order):
        offset = 0 if order == 0 else (-((order + 1) // 2) if order % 2 else order // 2)
        return lax.rem(z + (offset + RING), RING)

    def load_query_weight(order):
        column = pl.multiple_of(D + head_at(order) * HD, HD)
        return pltpu.make_async_copy(
            wuq_hbm.at[0, :, pl.ds(column, HD)], wq.at[order], wsem.at[order]
        )

    load_x = pltpu.make_async_copy(x_hbm, xv, lsem.at[0])
    load_wg = pltpu.make_async_copy(wuq_hbm.at[0, :, pl.ds(0, D)], wg, lsem.at[1])
    landed = (landed_a, landed_b)

    def half_rows(half):
        return pl.ds(half * (BLK // 2), BLK // 2)

    def load_own(half):
        return pltpu.make_async_copy(
            kv_hbm.at[0, 0, half_rows(half), pl.ds(column_of(me_c), HD)],
            landed[half].at[me_c],
            lsem.at[2 + half],
        )

    load_x.start()
    for order in range(H):
        load_query_weight(order).start()
    for half in range(2):
        load_own(half).start()
    load_wg.start()

    barrier = pltpu.get_barrier_semaphore()

    def greet(d, carry):
        pl.semaphore_signal(
            barrier, inc=1, device_id={"ctx": lax.rem(me_c + d, CTX)}, device_id_type=MESH
        )
        pl.semaphore_signal(
            barrier, inc=1, device_id={"users": lax.rem(me_u + d, USERS)}, device_id_type=MESH
        )
        return carry

    lax.fori_loop(1, 16, greet, 0)
    pl.semaphore_wait(barrier, 30)

    def send_blocks(half):
        def send(d, carry):
            dst = lax.rem(me_c + lax.rem(d * 7, CTX), CTX)
            pltpu.make_async_remote_copy(
                src_ref=kv_hbm.at[0, 0, half_rows(half), pl.ds(column_of(dst), HD)],
                dst_ref=landed[half].at[me_c],
                send_sem=a_send.at[half],
                recv_sem=a_recv.at[half],
                device_id={"ctx": dst},
                device_id_type=MESH,
            ).start()
            return carry

        lax.fori_loop(1, CTX, send, 0)

    def blocks_wait(half, sem):
        got = landed[half].at[pl.ds(0, CTX - 1)]
        pltpu.make_async_copy(got, got, sem.at[half]).wait()

    send_blocks(0)

    row_id = lax.broadcasted_iota(jnp.int32, (ROWS, ROWS), 0)
    col_id = lax.broadcasted_iota(jnp.int32, (ROWS, ROWS), 1)
    users = jnp.sum(
        jnp.where(row_id == col_id, usr_ref[...].astype(F32), 0.0), axis=1, keepdims=True
    )
    one_hot = (users == lax.broadcasted_iota(jnp.int32, (ROWS, 128), 1).astype(F32)).astype(F32)
    before = (col_id < row_id).astype(F32).astype(BF16)
    earlier = jnp.dot(before, one_hot.astype(BF16), preferred_element_type=F32)
    rank = jnp.sum(earlier * one_hot, axis=1, keepdims=True)
    slot = users * CAP + rank
    slot_row = jnp.sum(jnp.where(row_id == col_id, slot, 0.0), axis=0, keepdims=True)
    comb[...] = (
        (lax.broadcasted_iota(jnp.int32, (ROWS, SLOTS), 1).astype(F32) == slot)
        .astype(F32).astype(BF16)
    )
    disp[...] = (
        (lax.broadcasted_iota(jnp.int32, (SLOTS, ROWS), 0).astype(F32) == slot_row)
        .astype(F32).astype(BF16)
    )

    load_x.wait()

    def norm_rows(t, carry):
        rows = pl.ds(pl.multiple_of(t * 64, 64), 64)
        value = xv[rows, :].astype(F32)
        shifted = value - jnp.mean(value, axis=1, keepdims=True)
        spread = jnp.mean(shifted * shifted, axis=1, keepdims=True)
        normed[rows, :] = (shifted * lax.rsqrt(spread + 1e-05) * gin_ref[...]).astype(BF16)
        return carry

    lax.fori_loop(0, ROWS // 64, norm_rows, 0, unroll=True)
    def exchange(group, source, target, send_sem, recv_sem):
        first, count = group[0], len(group)

        def send(d, carry):
            dst = partner_user(me_u, d)
            pltpu.make_async_remote_copy(
                src_ref=source.at[pl.ds(first, count), slot_rows(dst), :],
                dst_ref=target.at[pl.ds(first, count), slot_rows(me_u), :],
                send_sem=send_sem,
                recv_sem=recv_sem,
                device_id={"users": dst},
                device_id_type=MESH,
            ).start()
            return carry

        lax.fori_loop(1, USERS, send, 0)
        for order in group:
            target[order, slot_rows(me_u), :] = source[order, slot_rows(me_u), :]

    def exchange_wait(group, buffer, sem):
        part = buffer.at[pl.ds(group[0], len(group)), pl.ds(0, SLOTS - CAP), :]
        pltpu.make_async_copy(part, part, sem).wait()

    def route_queries(g):
        group = GROUPS[g]
        for order in group:
            load_query_weight(order).wait()
        weights = [wq[order] for order in group]
        weight = weights[0] if len(group) == 1 else jnp.concatenate(weights, axis=1)
        query = silu(jnp.dot(normed[...], weight, preferred_element_type=F32)).astype(BF16)
        routed = jnp.dot(disp[...], query, preferred_element_type=F32).astype(BF16)
        for at, order in enumerate(group):
            qs[order] = routed[:, at * HD:(at + 1) * HD]

    def send_queries(g):
        exchange(GROUPS[g], qs, qr, q_send.at[g], q_recv.at[g])

    route_queries(0)
    send_queries(0)
    route_queries(1)
    send_queries(1)
    blocks_wait(0, a_send)
    send_blocks(1)
    route_queries(2)
    load_wg.wait()

    def project_gate(n, carry):
        cols = pl.ds(pl.multiple_of(n * 256, 256), 256)
        gate[:, cols] = silu(jnp.dot(normed[...], wg[:, cols], preferred_element_type=F32))
        return carry

    lax.fori_loop(0, H // 2, project_gate, 0)

    counts = []
    running = jnp.int32(0)
    for b in range(CTX):
        running = running + mask_ref[0, b]
        counts.append(running)
    live = []
    for r in range(LIVE):
        block = jnp.int32(0)
        for b in range(CTX):
            block = block + (counts[b] <= r).astype(jnp.int32)
        live.append(jnp.minimum(block, CTX - 1))

    def piece(lane, head, half):
        return lane * 2 * RING + head * 2 + half

    right = {"ctx": lax.rem(z + 1, RING) * 2 + core}
    left = {"ctx": lax.rem(z + RING - 1, RING) * 2 + core}
    sibling = {"ctx": z * 2 + 1 - core}

    def pass_on(at, to, send_sem, recv_sem):
        pltpu.make_async_remote_copy(
            src_ref=kv.at[at], dst_ref=kv.at[at], send_sem=send_sem, recv_sem=recv_sem,
            device_id=to, device_id_type=MESH,
        ).start()

    def arrived(at, sem):
        pltpu.make_async_copy(kv.at[at], kv.at[at], sem).wait()

    def quarter(at, sub):
        return at, pl.ds(sub * (HALF // 2), HALF // 2)

    def start_round(own, half, sub):
        pass_on(quarter(own, sub), right, r_send, r_recv.at[half, sub])
        pass_on(quarter(own, sub), left, l_send, l_recv.at[half, sub])

    for half in range(2):
        load_own(half).wait()
        blocks_wait(half, a_recv)
        own = piece(core, z, half)
        for r in range(LIVE):
            kv[own, pl.ds(r * (BLK // 2), BLK // 2), :] = landed[half][live[r]]
        start_round(own, half, 0)
        pass_on(own, sibling, s_send, so_recv.at[half])
        if half == 0:
            send_queries(2)
            route_queries(3)
            start_round(own, half, 1)
            route_queries(4)
        else:
            send_queries(3)
            send_queries(4)
            start_round(own, half, 1)

    scale = 0.5 * HD ** (-0.5)

    def attend(order, half, opening):
        head = head_at(order)
        scores = lax.dot_general(
            qr[order], kv[piece(0, head, half)], (((1,), (1,)), ((), ())),
            preferred_element_type=F32,
        ) * scale
        weights = (scores + scores * jnp.tanh(scores)).astype(BF16)
        value = jnp.dot(weights, kv[piece(1, head, half)], preferred_element_type=F32)
        if opening:
            acc[order] = value
        else:
            asend[order] = (acc[order] + value).astype(BF16)

    def send_attended(g):
        exchange(GROUPS[g], asend, arecv, t_send.at[g], t_recv.at[g])

    def finish_first():
        exchange_wait(GROUPS[0], qr, q_recv.at[0])
        for half in range(2):
            arrived(piece(1 - core, z, half), so_recv.at[half])
            attend(0, half, half == 0)
        send_attended(0)

    def units_of(i):
        s, first = i // 2 + 1, i % 2
        if s == 4:
            return ((7, 0), (7, 1))
        return ((2 * s - 1, first), (2 * s, first))

    def finish(i):
        s = i // 2 + 1
        opening = i % 2 == 0
        if opening:
            exchange_wait(GROUPS[s], qr, q_recv.at[s])
        (lo, lo_half), (hi, hi_half) = units_of(i)
        arrived(piece(1 - core, head_at(lo), lo_half), sr_recv.at[i])
        attend(lo, lo_half, opening)
        arrived(piece(1 - core, head_at(hi), hi_half), sl_recv.at[i])
        attend(hi, hi_half, opening and s < 4)
        if not opening or s == 4:
            send_attended(s)

    for i in range(7):
        (lo, lo_half), (hi, hi_half) = units_of(i)
        from_left = piece(core, head_at(lo), lo_half)
        from_right = piece(core, head_at(hi), hi_half)
        for sub in range(2):
            arrived(quarter(from_left, sub), r_recv.at[i, sub])
            if i < 5:
                pass_on(quarter(from_left, sub), right, r_send, r_recv.at[i + 2, sub])
            arrived(quarter(from_right, sub), l_recv.at[i, sub])
            if i < 4 or i == 5:
                pass_on(quarter(from_right, sub), left, l_send, l_recv.at[min(i + 2, 6), sub])
        pass_on(from_left, sibling, s_send, sr_recv.at[i])
        pass_on(from_right, sibling, s_send, sl_recv.at[i])
        if i == 0:
            finish_first()
        elif i < 6:
            finish(i - 1)
        if i == 5:
            finish(5)
    finish(6)

    for g, group in enumerate(GROUPS):
        exchange_wait(group, arecv, t_recv.at[g])
        parts = [arecv[order] for order in group]
        packed = parts[0] if len(group) == 1 else jnp.concatenate(parts, axis=1)
        own = jnp.dot(comb[...], packed, preferred_element_type=F32)
        for at, order in enumerate(group):
            att[head_at(order)] = own[:, at * HD:(at + 1) * HD]

    def mix_rows(t, carry):
        rows = pl.ds(pl.multiple_of(t * 64, 64), 64)
        value = jnp.concatenate([att[h, rows, :] for h in range(H)], axis=1)
        shifted = value - jnp.mean(value, axis=1, keepdims=True)
        spread = jnp.mean(shifted * shifted, axis=1, keepdims=True)
        mixed_ref[rows, :] = (
            shifted * lax.rsqrt(spread + 1e-05) * gattn_ref[...] * gate[rows, :]
        ).astype(BF16)
        return carry

    lax.fori_loop(0, ROWS // 64, mix_rows, 0, unroll=True)
    blocks_wait(1, a_send)
    for g, group in enumerate(GROUPS):
        exchange_wait(group, qs, q_send.at[g])
        exchange_wait(group, asend, t_send.at[g])
    for sem, count in ((r_send, 7), (l_send, 7), (s_send, 16)):
        moved = kv.at[pl.ds(0, count)]
        pltpu.make_async_copy(moved, moved, sem).wait()


def on_device(cand_feat, cand_user, hist_kv, hist_mask, gain_in, w_uq, gain_attn, w_out):
    anywhere = pl.BlockSpec(memory_space=pl.ANY)
    vmem = pl.BlockSpec(memory_space=pltpu.VMEM)
    dma = pltpu.SemaphoreType.DMA
    mixed = pl.pallas_call(
        kernel,
        out_shape=jax.ShapeDtypeStruct((ROWS, D), BF16),
        in_specs=[
            anywhere, vmem, anywhere, pl.BlockSpec(memory_space=pltpu.SMEM),
            vmem, anywhere, vmem,
        ],
        out_specs=vmem,
        scratch_shapes=[
            pltpu.VMEM((ROWS, D), BF16),
            pltpu.VMEM((H, D, HD), BF16),
            pltpu.VMEM((D, D), BF16),
            pltpu.VMEM((CTX, BLK // 2, HD), BF16),
            pltpu.VMEM((CTX, BLK // 2, HD), BF16),
            pltpu.VMEM((2 * 2 * RING, HALF, HD), BF16),
            pltpu.VMEM((ROWS, D), BF16),
            pltpu.VMEM((H, SLOTS, HD), BF16),
            pltpu.VMEM((H, SLOTS, HD), BF16),
            pltpu.VMEM((H, SLOTS, HD), BF16),
            pltpu.VMEM((H, SLOTS, HD), BF16),
            pltpu.VMEM((H, SLOTS, HD), F32),
            pltpu.VMEM((H, ROWS, HD), F32),
            pltpu.VMEM((ROWS, D), F32),
            pltpu.VMEM((SLOTS, ROWS), BF16),
            pltpu.VMEM((ROWS, SLOTS), BF16),
            dma((4,)), dma((H,)), dma((2,)), dma((2,)), dma((5,)), dma((5,)), dma((5,)), dma((5,)),
            dma(()), dma(()), dma(()), dma((7, 2)), dma((7, 2)), dma((2,)), dma((7,)), dma((7,)),
        ],
        compiler_params=pltpu.CompilerParams(
            collective_id=0, has_side_effects=True, vmem_limit_bytes=56 * 1024 * 1024
        ),
    )(cand_feat, cand_user.reshape(1, ROWS), hist_kv, hist_mask, gain_in, w_uq, gain_attn)
    scored = jnp.dot(mixed, w_out[0], preferred_element_type=F32)
    return (cand_feat.astype(F32) + scored).astype(BF16)


def solution(mesh):
    in_specs = (
        P(("users", "ctx"), None),
        P(("users", "ctx"), None),
        P(None, "users", "ctx", None),
        P("users", None),
        P(),
        P(),
        P(),
        P(),
    )
    out_specs = P(("users", "ctx"), None)
    return jax.shard_map(
        on_device, mesh=mesh, in_specs=in_specs, out_specs=out_specs, check_vma=False
    )
```

```python
import jax
import jax.numpy as jnp
from jax import lax
from jax.experimental import pallas as pl
from jax.experimental.pallas import tpu as pltpu
from jax.sharding import PartitionSpec as P

H = 8
HD = 128
D = H * HD
BLK = 128
LIVE = 8
ROWS = 384
USERS = 16
CTX = 16
RING = 8
CAP = 48
SLOTS = USERS * CAP
HALF = LIVE * BLK // 2
GROUPS = ((0,), (1, 2), (3, 4), (5, 6), (7,))
MESH = pl.DeviceIdType.MESH
F32 = jnp.float32
BF16 = jnp.bfloat16


def silu(v):
    half = 0.5 * v
    return half + half * jnp.tanh(half)


def partner_user(me_u, d):
    step = lax.rem(d * 7, USERS)
    nx = lax.rem(lax.div(me_u, 4) + lax.div(step, 4), 4)
    ny = lax.rem(lax.rem(me_u, 4) + lax.rem(step, 4), 4)
    return nx * 4 + ny


def slot_rows(user):
    return pl.ds(pl.multiple_of(user * CAP, CAP), CAP)


def kernel(
    x_hbm, usr_ref, kv_hbm, mask_ref, gin_ref, wuq_hbm, gattn_ref, mixed_ref,
    xv, wq, wg, landed_a, landed_b, kv, normed, qs, qr, asend, arecv, acc, att, gate, disp, comb,
    lsem, wsem, a_send, a_recv, q_send, q_recv, t_send, t_recv,
    r_send, l_send, s_send, r_recv, l_recv, so_recv, sr_recv, sl_recv,
):
    me_u = lax.axis_index("users")
    me_c = lax.axis_index("ctx")
    z = lax.div(me_c, 2)
    core = lax.rem(me_c, 2)

    def column_of(ctx):
        return pl.multiple_of(lax.rem(ctx, 2) * D + lax.div(ctx, 2) * HD, HD)

    def head_at(order):
        offset = 0 if order == 0 else (-((order + 1) // 2) if order % 2 else order // 2)
        return lax.rem(z + (offset + RING), RING)

    def load_query_weight(order):
        column = pl.multiple_of(D + head_at(order) * HD, HD)
        return pltpu.make_async_copy(
            wuq_hbm.at[0, :, pl.ds(column, HD)], wq.at[order], wsem.at[order]
        )

    load_x = pltpu.make_async_copy(x_hbm, xv, lsem.at[0])
    load_wg = pltpu.make_async_copy(wuq_hbm.at[0, :, pl.ds(0, D)], wg, lsem.at[1])
    landed = (landed_a, landed_b)

    def half_rows(half):
        return pl.ds(half * (BLK // 2), BLK // 2)

    def load_own(half):
        return pltpu.make_async_copy(
            kv_hbm.at[0, 0, half_rows(half), pl.ds(column_of(me_c), HD)],
            landed[half].at[me_c],
            lsem.at[2 + half],
        )

    load_x.start()
    for order in range(H):
        load_query_weight(order).start()
    for half in range(2):
        load_own(half).start()
    load_wg.start()

    barrier = pltpu.get_barrier_semaphore()

    def greet(d, carry):
        pl.semaphore_signal(
            barrier, inc=1, device_id={"ctx": lax.rem(me_c + d, CTX)}, device_id_type=MESH
        )
        pl.semaphore_signal(
            barrier, inc=1, device_id={"users": lax.rem(me_u + d, USERS)}, device_id_type=MESH
        )
        return carry

    lax.fori_loop(1, 16, greet, 0)
    pl.semaphore_wait(barrier, 30)

    def send_blocks(half):
        def send(d, carry):
            dst = lax.rem(me_c + lax.rem(d * 7, CTX), CTX)
            pltpu.make_async_remote_copy(
                src_ref=kv_hbm.at[0, 0, half_rows(half), pl.ds(column_of(dst), HD)],
                dst_ref=landed[half].at[me_c],
                send_sem=a_send.at[half],
                recv_sem=a_recv.at[half],
                device_id={"ctx": dst},
                device_id_type=MESH,
            ).start()
            return carry

        lax.fori_loop(1, CTX, send, 0)

    def blocks_wait(half, sem):
        got = landed[half].at[pl.ds(0, CTX - 1)]
        pltpu.make_async_copy(got, got, sem.at[half]).wait()

    send_blocks(0)

    row_id = lax.broadcasted_iota(jnp.int32, (ROWS, ROWS), 0)
    col_id = lax.broadcasted_iota(jnp.int32, (ROWS, ROWS), 1)
    users = jnp.sum(
        jnp.where(row_id == col_id, usr_ref[...].astype(F32), 0.0), axis=1, keepdims=True
    )
    one_hot = (users == lax.broadcasted_iota(jnp.int32, (ROWS, 128), 1).astype(F32)).astype(F32)
    before = (col_id < row_id).astype(F32).astype(BF16)
    earlier = jnp.dot(before, one_hot.astype(BF16), preferred_element_type=F32)
    rank = jnp.sum(earlier * one_hot, axis=1, keepdims=True)
    slot = users * CAP + rank
    slot_row = jnp.sum(jnp.where(row_id == col_id, slot, 0.0), axis=0, keepdims=True)
    comb[...] = (
        (lax.broadcasted_iota(jnp.int32, (ROWS, SLOTS), 1).astype(F32) == slot)
        .astype(F32).astype(BF16)
    )
    disp[...] = (
        (lax.broadcasted_iota(jnp.int32, (SLOTS, ROWS), 0).astype(F32) == slot_row)
        .astype(F32).astype(BF16)
    )

    load_x.wait()

    def norm_rows(t, carry):
        rows = pl.ds(pl.multiple_of(t * 64, 64), 64)
        value = xv[rows, :].astype(F32)
        shifted = value - jnp.mean(value, axis=1, keepdims=True)
        spread = jnp.mean(shifted * shifted, axis=1, keepdims=True)
        normed[rows, :] = (shifted * lax.rsqrt(spread + 1e-05) * gin_ref[...]).astype(BF16)
        return carry

    lax.fori_loop(0, ROWS // 64, norm_rows, 0, unroll=True)
    def exchange(group, source, target, send_sem, recv_sem):
        first, count = group[0], len(group)

        def send(d, carry):
            dst = partner_user(me_u, d)
            pltpu.make_async_remote_copy(
                src_ref=source.at[pl.ds(first, count), slot_rows(dst), :],
                dst_ref=target.at[pl.ds(first, count), slot_rows(me_u), :],
                send_sem=send_sem,
                recv_sem=recv_sem,
                device_id={"users": dst},
                device_id_type=MESH,
            ).start()
            return carry

        lax.fori_loop(1, USERS, send, 0)
        for order in group:
            target[order, slot_rows(me_u), :] = source[order, slot_rows(me_u), :]

    def exchange_wait(group, buffer, sem):
        part = buffer.at[pl.ds(group[0], len(group)), pl.ds(0, SLOTS - CAP), :]
        pltpu.make_async_copy(part, part, sem).wait()

    def route_queries(g):
        group = GROUPS[g]
        for order in group:
            load_query_weight(order).wait()
        weights = [wq[order] for order in group]
        weight = weights[0] if len(group) == 1 else jnp.concatenate(weights, axis=1)
        query = silu(jnp.dot(normed[...], weight, preferred_element_type=F32)).astype(BF16)
        routed = jnp.dot(disp[...], query, preferred_element_type=F32).astype(BF16)
        for at, order in enumerate(group):
            qs[order] = routed[:, at * HD:(at + 1) * HD]

    def send_queries(g):
        exchange(GROUPS[g], qs, qr, q_send.at[g], q_recv.at[g])

    route_queries(0)
    send_queries(0)
    route_queries(1)
    send_queries(1)
    blocks_wait(0, a_send)
    send_blocks(1)
    route_queries(2)
    load_wg.wait()

    def project_gate(n, carry):
        cols = pl.ds(pl.multiple_of(n * 256, 256), 256)
        gate[:, cols] = silu(jnp.dot(normed[...], wg[:, cols], preferred_element_type=F32))
        return carry

    lax.fori_loop(0, H // 2, project_gate, 0)

    counts = []
    running = jnp.int32(0)
    for b in range(CTX):
        running = running + mask_ref[0, b]
        counts.append(running)
    live = []
    for r in range(LIVE):
        block = jnp.int32(0)
        for b in range(CTX):
            block = block + (counts[b] <= r).astype(jnp.int32)
        live.append(jnp.minimum(block, CTX - 1))

    def piece(lane, head, half):
        return lane * 2 * RING + head * 2 + half

    right = {"ctx": lax.rem(z + 1, RING) * 2 + core}
    left = {"ctx": lax.rem(z + RING - 1, RING) * 2 + core}
    sibling = {"ctx": z * 2 + 1 - core}

    def pass_on(at, to, send_sem, recv_sem):
        pltpu.make_async_remote_copy(
            src_ref=kv.at[at], dst_ref=kv.at[at], send_sem=send_sem, recv_sem=recv_sem,
            device_id=to, device_id_type=MESH,
        ).start()

    def arrived(at, sem):
        pltpu.make_async_copy(kv.at[at], kv.at[at], sem).wait()

    def quarter(at, sub):
        return at, pl.ds(sub * (HALF // 2), HALF // 2)

    def start_round(own, half, sub):
        pass_on(quarter(own, sub), right, r_send, r_recv.at[half, sub])
        pass_on(quarter(own, sub), left, l_send, l_recv.at[half, sub])

    for half in range(2):
        load_own(half).wait()
        blocks_wait(half, a_recv)
        own = piece(core, z, half)
        for r in range(LIVE):
            kv[own, pl.ds(r * (BLK // 2), BLK // 2), :] = landed[half][live[r]]
        start_round(own, half, 0)
        pass_on(own, sibling, s_send, so_recv.at[half])
        if half == 0:
            send_queries(2)
            route_queries(3)
            start_round(own, half, 1)
            route_queries(4)
        else:
            send_queries(3)
            send_queries(4)
            start_round(own, half, 1)

    scale = 0.5 * HD ** (-0.5)

    def attend(order, half, opening):
        head = head_at(order)
        scores = lax.dot_general(
            qr[order], kv[piece(0, head, half)], (((1,), (1,)), ((), ())),
            preferred_element_type=F32,
        ) * scale
        weights = (scores + scores * jnp.tanh(scores)).astype(BF16)
        value = jnp.dot(weights, kv[piece(1, head, half)], preferred_element_type=F32)
        if opening:
            acc[order] = value
        else:
            asend[order] = (acc[order] + value).astype(BF16)

    def send_attended(g):
        exchange(GROUPS[g], asend, arecv, t_send.at[g], t_recv.at[g])

    def finish_first():
        exchange_wait(GROUPS[0], qr, q_recv.at[0])
        for half in range(2):
            arrived(piece(1 - core, z, half), so_recv.at[half])
            attend(0, half, half == 0)
        send_attended(0)

    def units_of(i):
        s, first = i // 2 + 1, i % 2
        if s == 4:
            return ((7, 0), (7, 1))
        return ((2 * s - 1, first), (2 * s, first))

    def finish(i):
        s = i // 2 + 1
        opening = i % 2 == 0
        if opening:
            exchange_wait(GROUPS[s], qr, q_recv.at[s])
        (lo, lo_half), (hi, hi_half) = units_of(i)
        arrived(piece(1 - core, head_at(lo), lo_half), sr_recv.at[i])
        attend(lo, lo_half, opening)
        arrived(piece(1 - core, head_at(hi), hi_half), sl_recv.at[i])
        attend(hi, hi_half, opening and s < 4)
        if not opening or s == 4:
            send_attended(s)

    for i in range(7):
        (lo, lo_half), (hi, hi_half) = units_of(i)
        from_left = piece(core, head_at(lo), lo_half)
        from_right = piece(core, head_at(hi), hi_half)
        for sub in range(2):
            arrived(quarter(from_left, sub), r_recv.at[i, sub])
            if i < 5:
                pass_on(quarter(from_left, sub), right, r_send, r_recv.at[i + 2, sub])
            arrived(quarter(from_right, sub), l_recv.at[i, sub])
            if i < 4 or i == 5:
                pass_on(quarter(from_right, sub), left, l_send, l_recv.at[min(i + 2, 6), sub])
        pass_on(from_left, sibling, s_send, sr_recv.at[i])
        pass_on(from_right, sibling, s_send, sl_recv.at[i])
        if i == 0:
            finish_first()
        finish(i)

    for g, group in enumerate(GROUPS):
        exchange_wait(group, arecv, t_recv.at[g])
        parts = [arecv[order] for order in group]
        packed = parts[0] if len(group) == 1 else jnp.concatenate(parts, axis=1)
        own = jnp.dot(comb[...], packed, preferred_element_type=F32)
        for at, order in enumerate(group):
            att[head_at(order)] = own[:, at * HD:(at + 1) * HD]

    def mix_rows(t, carry):
        rows = pl.ds(pl.multiple_of(t * 64, 64), 64)
        value = jnp.concatenate([att[h, rows, :] for h in range(H)], axis=1)
        shifted = value - jnp.mean(value, axis=1, keepdims=True)
        spread = jnp.mean(shifted * shifted, axis=1, keepdims=True)
        mixed_ref[rows, :] = (
            shifted * lax.rsqrt(spread + 1e-05) * gattn_ref[...] * gate[rows, :]
        ).astype(BF16)
        return carry

    lax.fori_loop(0, ROWS // 64, mix_rows, 0, unroll=True)
    blocks_wait(1, a_send)
    for g, group in enumerate(GROUPS):
        exchange_wait(group, qs, q_send.at[g])
        exchange_wait(group, asend, t_send.at[g])
    for sem, count in ((r_send, 7), (l_send, 7), (s_send, 16)):
        moved = kv.at[pl.ds(0, count)]
        pltpu.make_async_copy(moved, moved, sem).wait()


def on_device(cand_feat, cand_user, hist_kv, hist_mask, gain_in, w_uq, gain_attn, w_out):
    anywhere = pl.BlockSpec(memory_space=pl.ANY)
    vmem = pl.BlockSpec(memory_space=pltpu.VMEM)
    dma = pltpu.SemaphoreType.DMA
    mixed = pl.pallas_call(
        kernel,
        out_shape=jax.ShapeDtypeStruct((ROWS, D), BF16),
        in_specs=[
            anywhere, vmem, anywhere, pl.BlockSpec(memory_space=pltpu.SMEM),
            vmem, anywhere, vmem,
        ],
        out_specs=vmem,
        scratch_shapes=[
            pltpu.VMEM((ROWS, D), BF16),
            pltpu.VMEM((H, D, HD), BF16),
            pltpu.VMEM((D, D), BF16),
            pltpu.VMEM((CTX, BLK // 2, HD), BF16),
            pltpu.VMEM((CTX, BLK // 2, HD), BF16),
            pltpu.VMEM((2 * 2 * RING, HALF, HD), BF16),
            pltpu.VMEM((ROWS, D), BF16),
            pltpu.VMEM((H, SLOTS, HD), BF16),
            pltpu.VMEM((H, SLOTS, HD), BF16),
            pltpu.VMEM((H, SLOTS, HD), BF16),
            pltpu.VMEM((H, SLOTS, HD), BF16),
            pltpu.VMEM((H, SLOTS, HD), F32),
            pltpu.VMEM((H, ROWS, HD), F32),
            pltpu.VMEM((ROWS, D), F32),
            pltpu.VMEM((SLOTS, ROWS), BF16),
            pltpu.VMEM((ROWS, SLOTS), BF16),
            dma((4,)), dma((H,)), dma((2,)), dma((2,)), dma((5,)), dma((5,)), dma((5,)), dma((5,)),
            dma(()), dma(()), dma(()), dma((7, 2)), dma((7, 2)), dma((2,)), dma((7,)), dma((7,)),
        ],
        compiler_params=pltpu.CompilerParams(
            collective_id=0, has_side_effects=True, vmem_limit_bytes=56 * 1024 * 1024
        ),
    )(cand_feat, cand_user.reshape(1, ROWS), hist_kv, hist_mask, gain_in, w_uq, gain_attn)
    scored = jnp.dot(mixed, w_out[0], preferred_element_type=F32)
    return (cand_feat.astype(F32) + scored).astype(BF16)


def solution(mesh):
    in_specs = (
        P(("users", "ctx"), None),
        P(("users", "ctx"), None),
        P(None, "users", "ctx", None),
        P("users", None),
        P(),
        P(),
        P(),
        P(),
    )
    out_specs = P(("users", "ctx"), None)
    return jax.shard_map(
        on_device, mesh=mesh, in_specs=in_specs, out_specs=out_specs, check_vma=False
    )
```

```python
import jax
import jax.numpy as jnp
from jax import lax
from jax.experimental import pallas as pl
from jax.experimental.pallas import tpu as pltpu
from jax.sharding import PartitionSpec as P

H = 8
HD = 128
D = H * HD
BLK = 128
LIVE = 8
ROWS = 384
USERS = 16
CTX = 16
RING = 8
CAP = 48
SLOTS = USERS * CAP
HALF = LIVE * BLK // 2
GROUPS = ((0,), (1, 2), (3, 4), (5, 6), (7,))
MESH = pl.DeviceIdType.MESH
F32 = jnp.float32
BF16 = jnp.bfloat16


def silu(v):
    half = 0.5 * v
    return half + half * jnp.tanh(half)


def partner_user(me_u, d):
    step = lax.rem(d * 7, USERS)
    nx = lax.rem(lax.div(me_u, 4) + lax.div(step, 4), 4)
    ny = lax.rem(lax.rem(me_u, 4) + lax.rem(step, 4), 4)
    return nx * 4 + ny


def slot_rows(user):
    return pl.ds(pl.multiple_of(user * CAP, CAP), CAP)


def kernel(
    x_hbm, usr_ref, kv_hbm, mask_ref, gin_ref, wuq_hbm, gattn_ref, mixed_ref,
    xv, wq, wg, landed_a, landed_b, kv, normed, qs, qr, asend, arecv, acc, att, gate, disp, comb,
    lsem, wsem, a_send, a_recv, q_send, q_recv, t_send, t_recv,
    r_send, l_send, s_send, r_recv, l_recv, so_recv, sr_recv, sl_recv,
):
    me_u = lax.axis_index("users")
    me_c = lax.axis_index("ctx")
    z = lax.div(me_c, 2)
    core = lax.rem(me_c, 2)

    def column_of(ctx):
        return pl.multiple_of(lax.rem(ctx, 2) * D + lax.div(ctx, 2) * HD, HD)

    def head_at(order):
        offset = 0 if order == 0 else (-((order + 1) // 2) if order % 2 else order // 2)
        return lax.rem(z + (offset + RING), RING)

    def load_query_weight(order):
        column = pl.multiple_of(D + head_at(order) * HD, HD)
        return pltpu.make_async_copy(
            wuq_hbm.at[0, :, pl.ds(column, HD)], wq.at[order], wsem.at[order]
        )

    load_x = pltpu.make_async_copy(x_hbm, xv, lsem.at[0])
    load_wg = pltpu.make_async_copy(wuq_hbm.at[0, :, pl.ds(0, D)], wg, lsem.at[1])
    landed = (landed_a, landed_b)

    def half_rows(half):
        return pl.ds(half * (BLK // 2), BLK // 2)

    def load_own(half):
        return pltpu.make_async_copy(
            kv_hbm.at[0, 0, half_rows(half), pl.ds(column_of(me_c), HD)],
            landed[half].at[me_c],
            lsem.at[2 + half],
        )

    load_x.start()
    for order in range(H):
        load_query_weight(order).start()
    for half in range(2):
        load_own(half).start()
    load_wg.start()

    barrier = pltpu.get_barrier_semaphore()

    def greet(d, carry):
        pl.semaphore_signal(
            barrier, inc=1, device_id={"ctx": lax.rem(me_c + d, CTX)}, device_id_type=MESH
        )
        pl.semaphore_signal(
            barrier, inc=1, device_id={"users": lax.rem(me_u + d, USERS)}, device_id_type=MESH
        )
        return carry

    lax.fori_loop(1, 16, greet, 0)
    pl.semaphore_wait(barrier, 30)

    def send_blocks(half):
        def send(d, carry):
            dst = lax.rem(me_c + lax.rem(d * 7, CTX), CTX)
            pltpu.make_async_remote_copy(
                src_ref=kv_hbm.at[0, 0, half_rows(half), pl.ds(column_of(dst), HD)],
                dst_ref=landed[half].at[me_c],
                send_sem=a_send.at[half],
                recv_sem=a_recv.at[half],
                device_id={"ctx": dst},
                device_id_type=MESH,
            ).start()
            return carry

        lax.fori_loop(1, CTX, send, 0)

    def blocks_wait(half, sem):
        got = landed[half].at[pl.ds(0, CTX - 1)]
        pltpu.make_async_copy(got, got, sem.at[half]).wait()

    send_blocks(0)

    row_id = lax.broadcasted_iota(jnp.int32, (ROWS, ROWS), 0)
    col_id = lax.broadcasted_iota(jnp.int32, (ROWS, ROWS), 1)
    users = jnp.sum(
        jnp.where(row_id == col_id, usr_ref[...].astype(F32), 0.0), axis=1, keepdims=True
    )
    one_hot = (users == lax.broadcasted_iota(jnp.int32, (ROWS, 128), 1).astype(F32)).astype(F32)
    before = (col_id < row_id).astype(F32).astype(BF16)
    earlier = jnp.dot(before, one_hot.astype(BF16), preferred_element_type=F32)
    rank = jnp.sum(earlier * one_hot, axis=1, keepdims=True)
    slot = users * CAP + rank
    slot_row = jnp.sum(jnp.where(row_id == col_id, slot, 0.0), axis=0, keepdims=True)
    comb[...] = (
        (lax.broadcasted_iota(jnp.int32, (ROWS, SLOTS), 1).astype(F32) == slot)
        .astype(F32).astype(BF16)
    )
    disp[...] = (
        (lax.broadcasted_iota(jnp.int32, (SLOTS, ROWS), 0).astype(F32) == slot_row)
        .astype(F32).astype(BF16)
    )

    load_x.wait()

    def norm_rows(t, carry):
        rows = pl.ds(pl.multiple_of(t * 64, 64), 64)
        value = xv[rows, :].astype(F32)
        shifted = value - jnp.mean(value, axis=1, keepdims=True)
        spread = jnp.mean(shifted * shifted, axis=1, keepdims=True)
        normed[rows, :] = (shifted * lax.rsqrt(spread + 1e-05) * gin_ref[...]).astype(BF16)
        return carry

    lax.fori_loop(0, ROWS // 64, norm_rows, 0, unroll=True)
    def exchange(group, source, target, send_sem, recv_sem):
        first, count = group[0], len(group)

        def send(d, carry):
            dst = partner_user(me_u, d)
            pltpu.make_async_remote_copy(
                src_ref=source.at[pl.ds(first, count), slot_rows(dst), :],
                dst_ref=target.at[pl.ds(first, count), slot_rows(me_u), :],
                send_sem=send_sem,
                recv_sem=recv_sem,
                device_id={"users": dst},
                device_id_type=MESH,
            ).start()
            return carry

        lax.fori_loop(1, USERS, send, 0, unroll=True)
        for order in group:
            target[order, slot_rows(me_u), :] = source[order, slot_rows(me_u), :]

    def exchange_wait(group, buffer, sem):
        part = buffer.at[pl.ds(group[0], len(group)), pl.ds(0, SLOTS - CAP), :]
        pltpu.make_async_copy(part, part, sem).wait()

    def route_queries(g):
        group = GROUPS[g]
        for order in group:
            load_query_weight(order).wait()
        weights = [wq[order] for order in group]
        weight = weights[0] if len(group) == 1 else jnp.concatenate(weights, axis=1)
        query = silu(jnp.dot(normed[...], weight, preferred_element_type=F32)).astype(BF16)
        routed = jnp.dot(disp[...], query, preferred_element_type=F32).astype(BF16)
        for at, order in enumerate(group):
            qs[order] = routed[:, at * HD:(at + 1) * HD]

    def send_queries(g):
        exchange(GROUPS[g], qs, qr, q_send.at[g], q_recv.at[g])

    route_queries(0)
    send_queries(0)
    route_queries(1)
    send_queries(1)
    blocks_wait(0, a_send)
    send_blocks(1)
    route_queries(2)
    load_wg.wait()

    def project_gate(n, carry):
        cols = pl.ds(pl.multiple_of(n * 256, 256), 256)
        gate[:, cols] = silu(jnp.dot(normed[...], wg[:, cols], preferred_element_type=F32))
        return carry

    lax.fori_loop(0, H // 2, project_gate, 0)

    counts = []
    running = jnp.int32(0)
    for b in range(CTX):
        running = running + mask_ref[0, b]
        counts.append(running)
    live = []
    for r in range(LIVE):
        block = jnp.int32(0)
        for b in range(CTX):
            block = block + (counts[b] <= r).astype(jnp.int32)
        live.append(jnp.minimum(block, CTX - 1))

    def piece(lane, head, half):
        return lane * 2 * RING + head * 2 + half

    right = {"ctx": lax.rem(z + 1, RING) * 2 + core}
    left = {"ctx": lax.rem(z + RING - 1, RING) * 2 + core}
    sibling = {"ctx": z * 2 + 1 - core}

    def pass_on(at, to, send_sem, recv_sem):
        pltpu.make_async_remote_copy(
            src_ref=kv.at[at], dst_ref=kv.at[at], send_sem=send_sem, recv_sem=recv_sem,
            device_id=to, device_id_type=MESH,
        ).start()

    def arrived(at, sem):
        pltpu.make_async_copy(kv.at[at], kv.at[at], sem).wait()

    def quarter(at, sub):
        return at, pl.ds(sub * (HALF // 2), HALF // 2)

    def start_round(own, half, sub):
        pass_on(quarter(own, sub), right, r_send, r_recv.at[half, sub])
        pass_on(quarter(own, sub), left, l_send, l_recv.at[half, sub])

    for half in range(2):
        load_own(half).wait()
        blocks_wait(half, a_recv)
        own = piece(core, z, half)
        for r in range(LIVE):
            kv[own, pl.ds(r * (BLK // 2), BLK // 2), :] = landed[half][live[r]]
        start_round(own, half, 0)
        pass_on(own, sibling, s_send, so_recv.at[half])
        if half == 0:
            send_queries(2)
            route_queries(3)
            start_round(own, half, 1)
            route_queries(4)
        else:
            send_queries(3)
            send_queries(4)
            start_round(own, half, 1)

    scale = 0.5 * HD ** (-0.5)

    def attend(order, half, opening):
        head = head_at(order)
        scores = lax.dot_general(
            qr[order], kv[piece(0, head, half)], (((1,), (1,)), ((), ())),
            preferred_element_type=F32,
        ) * scale
        weights = (scores + scores * jnp.tanh(scores)).astype(BF16)
        value = jnp.dot(weights, kv[piece(1, head, half)], preferred_element_type=F32)
        if opening:
            acc[order] = value
        else:
            asend[order] = (acc[order] + value).astype(BF16)

    def send_attended(g):
        exchange(GROUPS[g], asend, arecv, t_send.at[g], t_recv.at[g])

    def finish_first():
        exchange_wait(GROUPS[0], qr, q_recv.at[0])
        for half in range(2):
            arrived(piece(1 - core, z, half), so_recv.at[half])
            attend(0, half, half == 0)
        send_attended(0)

    def units_of(i):
        s, first = i // 2 + 1, i % 2
        if s == 4:
            return ((7, 0), (7, 1))
        return ((2 * s - 1, first), (2 * s, first))

    def finish(i):
        s = i // 2 + 1
        opening = i % 2 == 0
        if opening:
            exchange_wait(GROUPS[s], qr, q_recv.at[s])
        (lo, lo_half), (hi, hi_half) = units_of(i)
        arrived(piece(1 - core, head_at(lo), lo_half), sr_recv.at[i])
        attend(lo, lo_half, opening)
        arrived(piece(1 - core, head_at(hi), hi_half), sl_recv.at[i])
        attend(hi, hi_half, opening and s < 4)
        if not opening or s == 4:
            send_attended(s)

    for i in range(7):
        (lo, lo_half), (hi, hi_half) = units_of(i)
        from_left = piece(core, head_at(lo), lo_half)
        from_right = piece(core, head_at(hi), hi_half)
        for sub in range(2):
            arrived(quarter(from_left, sub), r_recv.at[i, sub])
            if i < 5:
                pass_on(quarter(from_left, sub), right, r_send, r_recv.at[i + 2, sub])
            arrived(quarter(from_right, sub), l_recv.at[i, sub])
            if i < 4 or i == 5:
                pass_on(quarter(from_right, sub), left, l_send, l_recv.at[min(i + 2, 6), sub])
        pass_on(from_left, sibling, s_send, sr_recv.at[i])
        pass_on(from_right, sibling, s_send, sl_recv.at[i])
        if i == 0:
            finish_first()
        finish(i)

    for g, group in enumerate(GROUPS):
        exchange_wait(group, arecv, t_recv.at[g])
        parts = [arecv[order] for order in group]
        packed = parts[0] if len(group) == 1 else jnp.concatenate(parts, axis=1)
        own = jnp.dot(comb[...], packed, preferred_element_type=F32)
        for at, order in enumerate(group):
            att[head_at(order)] = own[:, at * HD:(at + 1) * HD]

    def mix_rows(t, carry):
        rows = pl.ds(pl.multiple_of(t * 64, 64), 64)
        value = jnp.concatenate([att[h, rows, :] for h in range(H)], axis=1)
        shifted = value - jnp.mean(value, axis=1, keepdims=True)
        spread = jnp.mean(shifted * shifted, axis=1, keepdims=True)
        mixed_ref[rows, :] = (
            shifted * lax.rsqrt(spread + 1e-05) * gattn_ref[...] * gate[rows, :]
        ).astype(BF16)
        return carry

    lax.fori_loop(0, ROWS // 64, mix_rows, 0, unroll=True)
    blocks_wait(1, a_send)
    for g, group in enumerate(GROUPS):
        exchange_wait(group, qs, q_send.at[g])
        exchange_wait(group, asend, t_send.at[g])
    for sem, count in ((r_send, 7), (l_send, 7), (s_send, 16)):
        moved = kv.at[pl.ds(0, count)]
        pltpu.make_async_copy(moved, moved, sem).wait()


def on_device(cand_feat, cand_user, hist_kv, hist_mask, gain_in, w_uq, gain_attn, w_out):
    anywhere = pl.BlockSpec(memory_space=pl.ANY)
    vmem = pl.BlockSpec(memory_space=pltpu.VMEM)
    dma = pltpu.SemaphoreType.DMA
    mixed = pl.pallas_call(
        kernel,
        out_shape=jax.ShapeDtypeStruct((ROWS, D), BF16),
        in_specs=[
            anywhere, vmem, anywhere, pl.BlockSpec(memory_space=pltpu.SMEM),
            vmem, anywhere, vmem,
        ],
        out_specs=vmem,
        scratch_shapes=[
            pltpu.VMEM((ROWS, D), BF16),
            pltpu.VMEM((H, D, HD), BF16),
            pltpu.VMEM((D, D), BF16),
            pltpu.VMEM((CTX, BLK // 2, HD), BF16),
            pltpu.VMEM((CTX, BLK // 2, HD), BF16),
            pltpu.VMEM((2 * 2 * RING, HALF, HD), BF16),
            pltpu.VMEM((ROWS, D), BF16),
            pltpu.VMEM((H, SLOTS, HD), BF16),
            pltpu.VMEM((H, SLOTS, HD), BF16),
            pltpu.VMEM((H, SLOTS, HD), BF16),
            pltpu.VMEM((H, SLOTS, HD), BF16),
            pltpu.VMEM((H, SLOTS, HD), F32),
            pltpu.VMEM((H, ROWS, HD), F32),
            pltpu.VMEM((ROWS, D), F32),
            pltpu.VMEM((SLOTS, ROWS), BF16),
            pltpu.VMEM((ROWS, SLOTS), BF16),
            dma((4,)), dma((H,)), dma((2,)), dma((2,)), dma((5,)), dma((5,)), dma((5,)), dma((5,)),
            dma(()), dma(()), dma(()), dma((7, 2)), dma((7, 2)), dma((2,)), dma((7,)), dma((7,)),
        ],
        compiler_params=pltpu.CompilerParams(
            collective_id=0, has_side_effects=True, vmem_limit_bytes=56 * 1024 * 1024
        ),
    )(cand_feat, cand_user.reshape(1, ROWS), hist_kv, hist_mask, gain_in, w_uq, gain_attn)
    scored = jnp.dot(mixed, w_out[0], preferred_element_type=F32)
    return (cand_feat.astype(F32) + scored).astype(BF16)


def solution(mesh):
    in_specs = (
        P(("users", "ctx"), None),
        P(("users", "ctx"), None),
        P(None, "users", "ctx", None),
        P("users", None),
        P(),
        P(),
        P(),
        P(),
    )
    out_specs = P(("users", "ctx"), None)
    return jax.shard_map(
        on_device, mesh=mesh, in_specs=in_specs, out_specs=out_specs, check_vma=False
    )
```

```python
import jax
import jax.numpy as jnp
from jax import lax
from jax.experimental import pallas as pl
from jax.experimental.pallas import tpu as pltpu
from jax.sharding import PartitionSpec as P

H = 8
HD = 128
D = H * HD
BLK = 128
LIVE = 8
ROWS = 384
USERS = 16
CTX = 16
RING = 8
CAP = 48
SLOTS = USERS * CAP
HALF = LIVE * BLK // 2
GROUPS = ((0,), (1, 2), (3, 4), (5, 6), (7,))
MESH = pl.DeviceIdType.MESH
F32 = jnp.float32
BF16 = jnp.bfloat16


def silu(v):
    half = 0.5 * v
    return half + half * jnp.tanh(half)


def partner_user(me_u, d):
    step = lax.rem(d * 7, USERS)
    nx = lax.rem(lax.div(me_u, 4) + lax.div(step, 4), 4)
    ny = lax.rem(lax.rem(me_u, 4) + lax.rem(step, 4), 4)
    return nx * 4 + ny


def slot_rows(user):
    return pl.ds(pl.multiple_of(user * CAP, CAP), CAP)


def kernel(
    x_hbm, usr_ref, kv_hbm, mask_ref, gin_ref, wuq_hbm, gattn_ref, mixed_ref,
    xv, wq, wg, landed_a, landed_b, kv, normed, qs, qr, asend, arecv, acc, att, gate, disp, comb,
    lsem, wsem, a_send, a_recv, q_send, q_recv, t_send, t_recv,
    r_send, l_send, s_send, r_recv, l_recv, so_recv, sr_recv, sl_recv,
):
    me_u = lax.axis_index("users")
    me_c = lax.axis_index("ctx")
    z = lax.div(me_c, 2)
    core = lax.rem(me_c, 2)

    def column_of(ctx):
        return pl.multiple_of(lax.rem(ctx, 2) * D + lax.div(ctx, 2) * HD, HD)

    def head_at(order):
        offset = 0 if order == 0 else (-((order + 1) // 2) if order % 2 else order // 2)
        return lax.rem(z + (offset + RING), RING)

    def load_query_weight(order):
        column = pl.multiple_of(D + head_at(order) * HD, HD)
        return pltpu.make_async_copy(
            wuq_hbm.at[0, :, pl.ds(column, HD)], wq.at[order], wsem.at[order]
        )

    load_x = pltpu.make_async_copy(x_hbm, xv, lsem.at[0])
    load_wg = pltpu.make_async_copy(wuq_hbm.at[0, :, pl.ds(0, D)], wg, lsem.at[1])
    landed = (landed_a, landed_b)

    def half_rows(half):
        return pl.ds(half * (BLK // 2), BLK // 2)

    def load_own(half):
        return pltpu.make_async_copy(
            kv_hbm.at[0, 0, half_rows(half), pl.ds(column_of(me_c), HD)],
            landed[half].at[me_c],
            lsem.at[2 + half],
        )

    barrier = pltpu.get_barrier_semaphore()

    def greet(d, carry):
        pl.semaphore_signal(
            barrier, inc=1, device_id={"ctx": lax.rem(me_c + d, CTX)}, device_id_type=MESH
        )
        pl.semaphore_signal(
            barrier, inc=1, device_id={"users": lax.rem(me_u + d, USERS)}, device_id_type=MESH
        )
        return carry

    lax.fori_loop(1, 16, greet, 0, unroll=True)
    load_x.start()
    load_query_weight(0).start()
    pl.semaphore_wait(barrier, 30)

    def send_blocks(half):
        def send(d, carry):
            dst = lax.rem(me_c + lax.rem(d * 7, CTX), CTX)
            pltpu.make_async_remote_copy(
                src_ref=kv_hbm.at[0, 0, half_rows(half), pl.ds(column_of(dst), HD)],
                dst_ref=landed[half].at[me_c],
                send_sem=a_send.at[half],
                recv_sem=a_recv.at[half],
                device_id={"ctx": dst},
                device_id_type=MESH,
            ).start()
            return carry

        lax.fori_loop(1, CTX, send, 0, unroll=True)

    def blocks_wait(half, sem):
        got = landed[half].at[pl.ds(0, CTX - 1)]
        pltpu.make_async_copy(got, got, sem.at[half]).wait()

    send_blocks(0)
    for order in range(1, H):
        load_query_weight(order).start()
    for half in range(2):
        load_own(half).start()
    load_wg.start()

    row_id = lax.broadcasted_iota(jnp.int32, (ROWS, ROWS), 0)
    col_id = lax.broadcasted_iota(jnp.int32, (ROWS, ROWS), 1)
    users = jnp.sum(
        jnp.where(row_id == col_id, usr_ref[...].astype(F32), 0.0), axis=1, keepdims=True
    )
    one_hot = (users == lax.broadcasted_iota(jnp.int32, (ROWS, 128), 1).astype(F32)).astype(F32)
    before = (col_id < row_id).astype(F32).astype(BF16)
    earlier = jnp.dot(before, one_hot.astype(BF16), preferred_element_type=F32)
    rank = jnp.sum(earlier * one_hot, axis=1, keepdims=True)
    slot = users * CAP + rank
    slot_row = jnp.sum(jnp.where(row_id == col_id, slot, 0.0), axis=0, keepdims=True)
    comb[...] = (
        (lax.broadcasted_iota(jnp.int32, (ROWS, SLOTS), 1).astype(F32) == slot)
        .astype(F32).astype(BF16)
    )
    disp[...] = (
        (lax.broadcasted_iota(jnp.int32, (SLOTS, ROWS), 0).astype(F32) == slot_row)
        .astype(F32).astype(BF16)
    )

    load_x.wait()

    def norm_rows(t, carry):
        rows = pl.ds(pl.multiple_of(t * 64, 64), 64)
        value = xv[rows, :].astype(F32)
        shifted = value - jnp.mean(value, axis=1, keepdims=True)
        spread = jnp.mean(shifted * shifted, axis=1, keepdims=True)
        normed[rows, :] = (shifted * lax.rsqrt(spread + 1e-05) * gin_ref[...]).astype(BF16)
        return carry

    lax.fori_loop(0, ROWS // 64, norm_rows, 0, unroll=True)
    def exchange(group, source, target, send_sem, recv_sem):
        first, count = group[0], len(group)

        def send(d, carry):
            dst = partner_user(me_u, d)
            pltpu.make_async_remote_copy(
                src_ref=source.at[pl.ds(first, count), slot_rows(dst), :],
                dst_ref=target.at[pl.ds(first, count), slot_rows(me_u), :],
                send_sem=send_sem,
                recv_sem=recv_sem,
                device_id={"users": dst},
                device_id_type=MESH,
            ).start()
            return carry

        lax.fori_loop(1, USERS, send, 0, unroll=True)
        for order in group:
            target[order, slot_rows(me_u), :] = source[order, slot_rows(me_u), :]

    def exchange_wait(group, buffer, sem):
        part = buffer.at[pl.ds(group[0], len(group)), pl.ds(0, SLOTS - CAP), :]
        pltpu.make_async_copy(part, part, sem).wait()

    def route_queries(g):
        group = GROUPS[g]
        for order in group:
            load_query_weight(order).wait()
        weights = [wq[order] for order in group]
        weight = weights[0] if len(group) == 1 else jnp.concatenate(weights, axis=1)
        query = silu(jnp.dot(normed[...], weight, preferred_element_type=F32)).astype(BF16)
        routed = jnp.dot(disp[...], query, preferred_element_type=F32).astype(BF16)
        for at, order in enumerate(group):
            qs[order] = routed[:, at * HD:(at + 1) * HD]

    def send_queries(g):
        exchange(GROUPS[g], qs, qr, q_send.at[g], q_recv.at[g])

    route_queries(0)
    send_queries(0)
    route_queries(1)
    send_queries(1)
    blocks_wait(0, a_send)
    send_blocks(1)
    route_queries(2)
    load_wg.wait()

    def project_gate(n, carry):
        cols = pl.ds(pl.multiple_of(n * 256, 256), 256)
        gate[:, cols] = silu(jnp.dot(normed[...], wg[:, cols], preferred_element_type=F32))
        return carry

    lax.fori_loop(0, H // 2, project_gate, 0)

    counts = []
    running = jnp.int32(0)
    for b in range(CTX):
        running = running + mask_ref[0, b]
        counts.append(running)
    live = []
    for r in range(LIVE):
        block = jnp.int32(0)
        for b in range(CTX):
            block = block + (counts[b] <= r).astype(jnp.int32)
        live.append(jnp.minimum(block, CTX - 1))

    def piece(lane, head, half):
        return lane * 2 * RING + head * 2 + half

    right = {"ctx": lax.rem(z + 1, RING) * 2 + core}
    left = {"ctx": lax.rem(z + RING - 1, RING) * 2 + core}
    sibling = {"ctx": z * 2 + 1 - core}

    def pass_on(at, to, send_sem, recv_sem):
        pltpu.make_async_remote_copy(
            src_ref=kv.at[at], dst_ref=kv.at[at], send_sem=send_sem, recv_sem=recv_sem,
            device_id=to, device_id_type=MESH,
        ).start()

    def arrived(at, sem):
        pltpu.make_async_copy(kv.at[at], kv.at[at], sem).wait()

    def quarter(at, sub):
        return at, pl.ds(sub * (HALF // 2), HALF // 2)

    def start_round(own, half, sub):
        pass_on(quarter(own, sub), right, r_send, r_recv.at[half, sub])
        pass_on(quarter(own, sub), left, l_send, l_recv.at[half, sub])

    for half in range(2):
        load_own(half).wait()
        blocks_wait(half, a_recv)
        own = piece(core, z, half)
        for r in range(LIVE):
            kv[own, pl.ds(r * (BLK // 2), BLK // 2), :] = landed[half][live[r]]
        start_round(own, half, 0)
        pass_on(own, sibling, s_send, so_recv.at[half])
        if half == 0:
            send_queries(2)
            route_queries(3)
            start_round(own, half, 1)
            route_queries(4)
        else:
            send_queries(3)
            send_queries(4)
            start_round(own, half, 1)

    scale = 0.5 * HD ** (-0.5)

    def attend(order, half, opening):
        head = head_at(order)
        scores = lax.dot_general(
            qr[order], kv[piece(0, head, half)], (((1,), (1,)), ((), ())),
            preferred_element_type=F32,
        ) * scale
        weights = (scores + scores * jnp.tanh(scores)).astype(BF16)
        value = jnp.dot(weights, kv[piece(1, head, half)], preferred_element_type=F32)
        if opening:
            acc[order] = value
        else:
            asend[order] = (acc[order] + value).astype(BF16)

    def send_attended(g):
        exchange(GROUPS[g], asend, arecv, t_send.at[g], t_recv.at[g])

    def finish_first():
        exchange_wait(GROUPS[0], qr, q_recv.at[0])
        for half in range(2):
            arrived(piece(1 - core, z, half), so_recv.at[half])
            attend(0, half, half == 0)
        send_attended(0)

    def units_of(i):
        s, first = i // 2 + 1, i % 2
        if s == 4:
            return ((7, 0), (7, 1))
        return ((2 * s - 1, first), (2 * s, first))

    def finish(i):
        s = i // 2 + 1
        opening = i % 2 == 0
        if opening:
            exchange_wait(GROUPS[s], qr, q_recv.at[s])
        (lo, lo_half), (hi, hi_half) = units_of(i)
        for sub in range(2):
            arrived(quarter(piece(1 - core, head_at(lo), lo_half), sub), sr_recv.at[i, sub])
        attend(lo, lo_half, opening)
        for sub in range(2):
            arrived(quarter(piece(1 - core, head_at(hi), hi_half), sub), sl_recv.at[i, sub])
        attend(hi, hi_half, opening and s < 4)
        if not opening or s == 4:
            send_attended(s)

    for i in range(7):
        (lo, lo_half), (hi, hi_half) = units_of(i)
        from_left = piece(core, head_at(lo), lo_half)
        from_right = piece(core, head_at(hi), hi_half)
        for sub in range(2):
            arrived(quarter(from_left, sub), r_recv.at[i, sub])
            if i < 5:
                pass_on(quarter(from_left, sub), right, r_send, r_recv.at[i + 2, sub])
            pass_on(quarter(from_left, sub), sibling, s_send, sr_recv.at[i, sub])
            arrived(quarter(from_right, sub), l_recv.at[i, sub])
            if i < 4 or i == 5:
                pass_on(quarter(from_right, sub), left, l_send, l_recv.at[min(i + 2, 6), sub])
            pass_on(quarter(from_right, sub), sibling, s_send, sl_recv.at[i, sub])
        if i == 0:
            finish_first()
        finish(i)

    for g, group in enumerate(GROUPS):
        exchange_wait(group, arecv, t_recv.at[g])
        parts = [arecv[order] for order in group]
        packed = parts[0] if len(group) == 1 else jnp.concatenate(parts, axis=1)
        own = jnp.dot(comb[...], packed, preferred_element_type=F32)
        for at, order in enumerate(group):
            att[head_at(order)] = own[:, at * HD:(at + 1) * HD]

    def mix_rows(t, carry):
        rows = pl.ds(pl.multiple_of(t * 64, 64), 64)
        value = jnp.concatenate([att[h, rows, :] for h in range(H)], axis=1)
        shifted = value - jnp.mean(value, axis=1, keepdims=True)
        spread = jnp.mean(shifted * shifted, axis=1, keepdims=True)
        mixed_ref[rows, :] = (
            shifted * lax.rsqrt(spread + 1e-05) * gattn_ref[...] * gate[rows, :]
        ).astype(BF16)
        return carry

    lax.fori_loop(0, ROWS // 64, mix_rows, 0, unroll=True)
    blocks_wait(1, a_send)
    for g, group in enumerate(GROUPS):
        exchange_wait(group, qs, q_send.at[g])
        exchange_wait(group, asend, t_send.at[g])
    for sem, count in ((r_send, 7), (l_send, 7), (s_send, 16)):
        moved = kv.at[pl.ds(0, count)]
        pltpu.make_async_copy(moved, moved, sem).wait()


def on_device(cand_feat, cand_user, hist_kv, hist_mask, gain_in, w_uq, gain_attn, w_out):
    anywhere = pl.BlockSpec(memory_space=pl.ANY)
    vmem = pl.BlockSpec(memory_space=pltpu.VMEM)
    dma = pltpu.SemaphoreType.DMA
    mixed = pl.pallas_call(
        kernel,
        out_shape=jax.ShapeDtypeStruct((ROWS, D), BF16),
        in_specs=[
            anywhere, vmem, anywhere, pl.BlockSpec(memory_space=pltpu.SMEM),
            vmem, anywhere, vmem,
        ],
        out_specs=vmem,
        scratch_shapes=[
            pltpu.VMEM((ROWS, D), BF16),
            pltpu.VMEM((H, D, HD), BF16),
            pltpu.VMEM((D, D), BF16),
            pltpu.VMEM((CTX, BLK // 2, HD), BF16),
            pltpu.VMEM((CTX, BLK // 2, HD), BF16),
            pltpu.VMEM((2 * 2 * RING, HALF, HD), BF16),
            pltpu.VMEM((ROWS, D), BF16),
            pltpu.VMEM((H, SLOTS, HD), BF16),
            pltpu.VMEM((H, SLOTS, HD), BF16),
            pltpu.VMEM((H, SLOTS, HD), BF16),
            pltpu.VMEM((H, SLOTS, HD), BF16),
            pltpu.VMEM((H, SLOTS, HD), F32),
            pltpu.VMEM((H, ROWS, HD), F32),
            pltpu.VMEM((ROWS, D), F32),
            pltpu.VMEM((SLOTS, ROWS), BF16),
            pltpu.VMEM((ROWS, SLOTS), BF16),
            dma((4,)), dma((H,)), dma((2,)), dma((2,)), dma((5,)), dma((5,)), dma((5,)), dma((5,)),
            dma(()), dma(()), dma(()), dma((7, 2)), dma((7, 2)), dma((2,)), dma((7, 2)), dma((7, 2)),
        ],
        compiler_params=pltpu.CompilerParams(
            collective_id=0, has_side_effects=True, vmem_limit_bytes=56 * 1024 * 1024
        ),
    )(cand_feat, cand_user.reshape(1, ROWS), hist_kv, hist_mask, gain_in, w_uq, gain_attn)
    scored = jnp.dot(mixed, w_out[0], preferred_element_type=F32)
    return (cand_feat.astype(F32) + scored).astype(BF16)


def solution(mesh):
    in_specs = (
        P(("users", "ctx"), None),
        P(("users", "ctx"), None),
        P(None, "users", "ctx", None),
        P("users", None),
        P(),
        P(),
        P(),
        P(),
    )
    out_specs = P(("users", "ctx"), None)
    return jax.shard_map(
        on_device, mesh=mesh, in_specs=in_specs, out_specs=out_specs, check_vma=False
    )
```
